128 devices in a mesh: segment: 4 (over z), tok: 16 (over y, x), head: 2 (over core).
Axes of the slice: x: 4, y: 4, z: 4, core: 2. Of those that a mesh axis runs over, the one named last changes fastest.
Arguments:
- stream: float32 [2, 2048, 2048], P(None, 'tok', 'head'), may hold values from -6 to 6
- counts: int32 [4], replicated, may hold values from 1 to 2, as said below
- norm_gain: float32 [4, 2, 2048], P('segment'), may hold values from 0.5 to 1.5
- w_qkv: bfloat16 [4, 2, 2048, 3072], P('segment', None, None, 'head'), may hold values from -0.125 to 0.125
- w_out: bfloat16 [4, 2, 1024, 2048], P('segment', None, 'head'), may hold values from -0.1875 to 0.1875
- fast_init: float32 [4, 2, 2, 3, 512, 512], P('segment', None, 'head'), may hold values from -6 to 6
Outputs:
- section_out: float32 [4, 2, 2048, 2048], P('segment', None, 'tok', 'head')
- fast_final: float32 [4, 2, 2, 3, 512, 512], P('segment', None, 'head', None, 'tok')
The draws below stay inside these ranges and needn't reach their ends.
Inputs may be any that keep to these rules, and one draw needn't show every extreme that they name: `counts`: every section runs either 1 or 2 layers; some section runs 2 layers and some other section runs 1.
All inputs are finite; a program needn't handle non-finite values.
Results may differ from the reference program's by a relative error of at most 0.03.
Values sent between devices are 32-bit elements; how exact they have to be, the bound alone decides.
A program may use at most 128 MiB of HBM per device.

```python
import jax
import jax.numpy as jnp
from jax import lax

D = 2048
HEADS = 2
HD = 512
FH = 512
LMAX = 2
SPANS = 2
TOKENS = 2048
N_SEGMENT = 4


def draw_counts(key, part):
    pattern_key = jax.random.fold_in(key, 71)
    pattern = jax.random.randint(pattern_key, (), 1, 2 ** N_SEGMENT - 1)
    powers = 2 ** jnp.arange(N_SEGMENT, dtype=jnp.int32)
    picked = pattern // powers % 2
    layer_counts = 1 + picked * (LMAX - 1)
    return layer_counts.astype(jnp.int32)


def levels(rng, dims, shards, least, largest):
    gain, own = 1.0, jax.random.fold_in(rng, 6)
    for dim, shards_of in shards:
        heights = jnp.exp(jax.random.uniform(jax.random.fold_in(own, dim), (shards_of,), jnp.float32, least / len(shards), largest / len(shards)))
        gain = gain * jnp.repeat(heights, dims[dim] // shards_of).reshape([-1 if axis == dim else 1 for axis in range(len(dims))])
    return gain


def normal_values(stream_key, shape, width, most, pieces=(), held_as=jnp.bfloat16):
    result = width * jax.random.normal(stream_key, shape, jnp.float32)
    if pieces:
        result = result * levels(stream_key, shape, pieces, -0.22, 0.18)
    return jnp.clip(result, -most, most).astype(held_as)


def setup_inputs(seed: int = 0) -> dict:
    arg_keys = jax.random.split(jax.random.key(seed), 7)
    stream = normal_values(arg_keys[0], (SPANS, TOKENS, D), 1.0, 6.0, ((1, 16), (2, 2)), jnp.float32)
    counts = draw_counts(jax.random.fold_in(arg_keys[6], 71), 0)
    norm_gain = jnp.clip(1.0 + 0.1 * jax.random.normal(arg_keys[2], (N_SEGMENT, LMAX, D), jnp.float32), 0.5, 1.5)
    w_qkv = normal_values(arg_keys[3], (N_SEGMENT, LMAX, D, HEADS * 3 * HD), D ** -0.5, 0.125, ((0, 4), (3, 2)))
    w_out = normal_values(arg_keys[4], (N_SEGMENT, LMAX, HEADS * HD, D), (HEADS * HD) ** -0.5, 0.1875, ((0, 4), (2, 2)))
    fast_init = normal_values(arg_keys[5], (N_SEGMENT, LMAX, HEADS, 3, HD, FH), 1.0, 6.0, ((0, 4), (2, 2)), jnp.float32)
    return dict(stream=stream, counts=counts, norm_gain=norm_gain, w_qkv=w_qkv, w_out=w_out, fast_init=fast_init)


step_rate = 0.5
tiny = 1e-06

def rms_scale(values):
    return lax.rsqrt(lax.optimization_barrier(jnp.mean(values * values, axis=-1, keepdims=True)) + tiny)

def round_half(values):
    return lax.optimization_barrier(values.astype(jnp.bfloat16)).astype(jnp.float32)

def silu_slope(pre_gate):
    logistic = jax.nn.sigmoid(pre_gate)
    return logistic * (1.0 + pre_gate * (1.0 - logistic))

def contract(form, left, right):
    return jnp.einsum(form, left, right, precision=lax.Precision.HIGHEST)

def run_layer(rows_in, gain_row, qkv_layer, out_layer, fast_layer):
    token_count = rows_in.shape[0]
    widened = rows_in.astype(jnp.float32)
    normed = (widened * rms_scale(widened) * gain_row).astype(jnp.bfloat16)
    projected = round_half(jnp.dot(normed, qkv_layer, preferred_element_type=jnp.float32))
    projected = projected.reshape(token_count, HEADS, 3, HD)
    query_rows = projected[:, :, 0]
    key_rows = projected[:, :, 1]
    value_rows = projected[:, :, 2]
    head_scale = HD ** (-0.5)
    weights = round_half(fast_layer)
    w_first = weights[:, 0]
    w_third = weights[:, 1]
    w_second = weights[:, 2]
    gate_query = contract('thd,hdf->thf', query_rows, w_first) * head_scale
    lift_query = contract('thd,hdf->thf', query_rows, w_third) * head_scale
    hidden_query = round_half(jax.nn.silu(gate_query) * lift_query)
    answer = contract('thf,hdf->thd', hidden_query, w_second) * head_scale
    normed_out = round_half(answer * rms_scale(answer))
    flat_out = normed_out.reshape(token_count, HEADS * HD)
    summed = contract('tk,kd->td', flat_out, out_layer.astype(jnp.float32))
    rows_out = widened + summed
    gate_key = contract('thd,hdf->thf', key_rows, w_first) * head_scale
    lift_key = contract('thd,hdf->thf', key_rows, w_third) * head_scale
    gate_act = jax.nn.silu(gate_key)
    hidden_key = round_half(gate_act * lift_key)
    upstream = -head_scale * contract('thd,hdf->thf', value_rows, w_second)
    grad_gate = round_half(upstream * lift_key * silu_slope(gate_key))
    grad_lift = round_half(upstream * gate_act)
    grad_first = head_scale * contract('thd,thf->hdf', key_rows, grad_gate)
    grad_third = head_scale * contract('thd,thf->hdf', key_rows, grad_lift)
    grad_second = -head_scale * contract('thd,thf->hdf', value_rows, hidden_key)
    grad_total = jnp.stack([grad_first, grad_third, grad_second], axis=1)
    mean_square = lax.optimization_barrier(jnp.mean(grad_total * grad_total, axis=(2, 3), keepdims=True))
    updated = fast_layer - step_rate * grad_total * lax.rsqrt(mean_square + tiny)
    return (rows_out, updated)

def reference(stream, counts, norm_gain, w_qkv, w_out, fast_init):
    fast_states = [fast_init[index] for index in range(N_SEGMENT)]
    produced = [[] for index in range(N_SEGMENT)]
    for span_index in range(SPANS):
        rows_now = stream[span_index]
        for segment_index in range(N_SEGMENT):
            gains = norm_gain[segment_index]
            qkv_weights = w_qkv[segment_index]
            out_weights = w_out[segment_index]

            def layer_step(layer_index, state_pair):
                rows_in, fast_state = state_pair
                gain_row = lax.dynamic_index_in_dim(gains, layer_index, 0, keepdims=False)
                qkv_layer = lax.dynamic_index_in_dim(qkv_weights, layer_index, 0, keepdims=False)
                out_layer = lax.dynamic_index_in_dim(out_weights, layer_index, 0, keepdims=False)
                fast_layer = lax.dynamic_index_in_dim(fast_state, layer_index, 0, keepdims=False)
                rows_out, updated = run_layer(rows_in, gain_row, qkv_layer, out_layer, fast_layer)
                fast_state = lax.dynamic_update_index_in_dim(fast_state, updated, layer_index, 0)
                return (rows_out, fast_state)
            rows_now, fast_states[segment_index] = lax.fori_loop(0, counts[segment_index], layer_step, (rows_now, fast_states[segment_index]))
            produced[segment_index].append(rows_now)
    section_out = jnp.stack([jnp.stack(span_rows) for span_rows in produced])
    fast_final = jnp.stack(fast_states)
    return (section_out, fast_final)
```

```python
import functools

import jax
import jax.numpy as jnp
from jax import lax
from jax.experimental import pallas as pl
from jax.experimental.pallas import tpu as pltpu
from jax.sharding import PartitionSpec as P

MESH = pl.DeviceIdType.MESH
step_rate = 0.5
tiny = 1e-06
SIDE = 4
QUARTERS = 4
CHUNKS = 4

f32 = jnp.float32
bf16 = jnp.bfloat16


def kernel(
    stream, counts, gain, wqkv_hbm, wout_hbm, fast_hbm,
    res, fin,
    wqkv, wout, wfast, wb, xin, nbuf, psend, precv, kv, hk_ga_gb,
    gq, gt, r1, s1, r2, st, st_recv,
    load_sem, x_send, x_recv, z_send, z_recv, p_send, p_recv,
    rs1_send, rs1_recv, rs2_send, rs2_recv, ag1_send, ag1_recv, ag2_send, ag2_recv,
    st_send_sem, st_recv_sem, out_sem,
):
    sections = lax.axis_size("segment")
    s = lax.axis_index("segment")
    t = lax.axis_index("tok")
    h = lax.axis_index("head")
    iy = t // SIDE
    ix = t % SIDE
    rows = stream.shape[1]
    width = 2 * stream.shape[2]
    hd = wout.shape[1]
    chunk_rows = rows // CHUNKS
    chunk_cols = width // CHUNKS
    head_scale = hd ** (-0.5)

    def turn(i, d):
        return (i + d + SIDE) % SIDE

    def on_x(d):
        return {"tok": iy * SIDE + turn(ix, d)}

    def on_y(d):
        return {"tok": turn(iy, d) * SIDE + ix}

    partner = {"head": 1 - h}
    above = {"segment": (s + 1) % sections}
    below = {"segment": (s + sections - 1) % sections}

    def load(kind, slot):
        src, dst = ((wqkv_hbm, wqkv), (fast_hbm, wfast), (wout_hbm, wout))[kind]
        return pltpu.make_async_copy(src.at[slot], dst.at[slot], load_sem.at[kind, slot])

    def load_x(span):
        return pltpu.make_async_copy(stream.at[span], xin.at[span, h], load_sem.at[3, span])

    @pl.when(s == 0)
    def _():
        load_x(0).start()
        load_x(1).start()

    for slot in range(2):
        for kind in range(3):
            load(kind, slot).start()

    barrier = pltpu.get_barrier_semaphore()
    peers = [partner, above, below]
    for d in (1, 2, 3):
        peers += [on_x(d), on_y(d)]
    for peer in peers:
        pl.semaphore_signal(barrier, inc=1, device_id=peer, device_id_type=MESH)
    pl.semaphore_wait(barrier, len(peers))

    def remote(src, dst, send, recv, device):
        return pltpu.make_async_remote_copy(
            src_ref=src, dst_ref=dst, send_sem=send, recv_sem=recv,
            device_id=device, device_id_type=MESH,
        )

    def rows_of(c):
        return pl.ds(c * chunk_rows, chunk_rows)

    def hand_up(span, c):
        part = xin.at[span, h, rows_of(c)]
        return remote(part, part, z_send.at[span, c], z_recv.at[span, c], above)

    def share(span, c):
        part = xin.at[span, h, rows_of(c)]
        return remote(part, part, x_send.at[span, c], x_recv.at[span, c], partner)

    def share_in(span, c):
        part = xin.at[span, 1 - h, rows_of(c)]
        return remote(part, part, x_send.at[span, c], x_recv.at[span, c], partner)

    def mix(slot, c):
        return remote(
            psend.at[slot, c], precv.at[slot, c], p_send.at[slot, c], p_recv.at[slot, c], partner
        )

    def order(q):
        forward = 1 if q % 2 == 0 else -1
        if q < 2:
            return forward, iy, on_y, ix, on_x
        return forward, ix, on_x, iy, on_y

    def first_block(buf, slot, q, j):
        return buf.at[slot, q, :, j] if q < 2 else buf.at[slot, q, :, :, j]

    def own_block(buf, slot, q, j):
        if q < 2:
            return buf.at[slot, q, :, iy, j]
        return buf.at[slot, q, :, j, ix]

    def rs1(slot, q, k):
        d, i, to, _, _ = order(q)
        j = (turn(i, 2), turn(i, d), turn(i, -d))[k]
        return remote(
            first_block(gq, slot, q, j), r1.at[slot, q, k],
            rs1_send.at[slot, q, k], rs1_recv.at[slot, q, k], to(d if k < 2 else -d),
        )

    def rs2(slot, q, k):
        d, _, _, i, to = order(q)
        j = (turn(i, 2), turn(i, d), turn(i, -d))[k]
        return remote(
            s1.at[slot, q, :, j], r2.at[slot, q, k],
            rs2_send.at[slot, q, k], rs2_recv.at[slot, q, k], to(d if k < 2 else -d),
        )

    def ag1(slot, q, k):
        d, _, _, i, to = order(q)
        part = own_block(gt, slot, q, (i, i, turn(i, -d))[k])
        return remote(
            part, part, ag1_send.at[slot, q, k], ag1_recv.at[slot, q, k], to((d, -d, d)[k])
        )

    def ag2(slot, q, k):
        d, i, to, _, _ = order(q)
        part = first_block(gt, slot, q, (i, i, turn(i, -d))[k])
        return remote(
            part, part, ag2_send.at[slot, q, k], ag2_recv.at[slot, q, k], to((d, -d, d)[k])
        )

    def ag1_in(slot, q, k):
        d, _, _, i, to = order(q)
        part = own_block(gt, slot, q, (turn(i, -d), turn(i, d), turn(i, 2))[k])
        return remote(
            part, part, ag1_send.at[slot, q, k], ag1_recv.at[slot, q, k], to((d, -d, d)[k])
        )

    def ag2_in(slot, q, k):
        d, i, to, _, _ = order(q)
        part = first_block(gt, slot, q, (turn(i, -d), turn(i, d), turn(i, 2))[k])
        return remote(
            part, part, ag2_send.at[slot, q, k], ag2_recv.at[slot, q, k], to((d, -d, d)[k])
        )

    def rs1_open(slot):
        for k in (0, 2):
            for q in range(QUARTERS):
                rs1(slot, q, k).start()

    def rs1_pass(slot):
        for q in range(QUARTERS):
            d, i, _, _, _ = order(q)
            rs1(slot, q, 0).wait_recv()
            block = first_block(gq, slot, q, turn(i, d))
            block[...] = block[...] + r1[slot, q, 0]
            rs1(slot, q, 1).start()

    def rs1_close(slot):
        for q in range(QUARTERS):
            d, i, _, _, _ = order(q)
            rs1(slot, q, 2).wait_recv()
            rs1(slot, q, 1).wait_recv()
            s1[slot, q] = first_block(gq, slot, q, i)[...] + r1[slot, q, 1] + r1[slot, q, 2]
            rs2(slot, q, 0).start()
            rs2(slot, q, 2).start()

    def rs2_pass(slot):
        for q in range(QUARTERS):
            d, _, _, i, _ = order(q)
            rs2(slot, q, 0).wait_recv()
            block = s1.at[slot, q, :, turn(i, d)]
            block[...] = block[...] + r2[slot, q, 0]
            rs2(slot, q, 1).start()

    def rs2_close(slot):
        for q in range(QUARTERS):
            _, _, _, i, _ = order(q)
            rs2(slot, q, 2).wait_recv()
            rs2(slot, q, 1).wait_recv()
            own_block(gt, slot, q, i)[...] = s1[slot, q, :, i] + r2[slot, q, 1] + r2[slot, q, 2]

    def rs_sent(slot):
        for q in range(QUARTERS):
            for k in range(3):
                rs1(slot, q, k).wait_send()
                rs2(slot, q, k).wait_send()

    def ag_open(ag, slot):
        for q in range(QUARTERS):
            ag(slot, q, 0).start()
            ag(slot, q, 1).start()

    def ag_pass(ag, ag_in, slot):
        for q in range(QUARTERS):
            ag_in(slot, q, 0).wait_recv()
            ag(slot, q, 2).start()

    def ag_close(ag, ag_in, slot):
        for q in range(QUARTERS):
            ag_in(slot, q, 1).wait_recv()
            ag_in(slot, q, 2).wait_recv()

    def ag_sent(slot):
        for q in range(QUARTERS):
            for k in range(3):
                ag1(slot, q, k).wait_send()
                ag2(slot, q, k).wait_send()

    def kept(slot, shape):
        return jnp.broadcast_to(counts[s], shape) > slot

    def update_weights(slot):
        for m in range(3):

            def squares(b, total):
                part = total
                for q in range(QUARTERS):
                    values = gt[slot, q, m, b]
                    part = part + jnp.sum(values * values, axis=0)
                return part

            total = lax.fori_loop(0, SIDE, squares, jnp.zeros(gt.shape[-2:], f32))
            mean = jnp.sum(total, keepdims=True) / (hd * hd)
            factor = step_rate * lax.rsqrt(mean + tiny)

            def change(b, carry):
                for q in range(QUARTERS):
                    cols = pl.ds(q * 128, 128)
                    old = wfast[slot, m, pl.ds(b * SIDE, SIDE), :, cols]
                    new = old - factor * gt[slot, q, m, b]
                    wfast[slot, m, pl.ds(b * SIDE, SIDE), :, cols] = jnp.where(
                        kept(slot, new.shape), new, old
                    )
                return carry

            lax.fori_loop(0, SIDE, change, 0)

    def round_weights(slot):
        for m in range(3):

            def one(b, carry):
                block = wfast[slot, m, pl.ds(b * SIDE, SIDE)]
                height = SIDE * block.shape[1]
                wb[slot, m, pl.ds(b * height, height)] = block.reshape(height, hd).astype(bf16)
                return carry

            lax.fori_loop(0, SIDE, one, 0)

    def dot(a, b, dims=((1,), (0,))):
        return lax.dot_general(a, b, (dims, ((), ())), preferred_element_type=f32)

    def layer(span, slot):
        low = xin[span, 0]
        high = xin[span, 1]
        half = width // 2
        mean = (
            jnp.sum(low * low, axis=-1, keepdims=True) + jnp.sum(high * high, axis=-1, keepdims=True)
        ) / width
        scale = lax.rsqrt(mean + tiny)
        gains = gain[slot]
        nbuf[:, :half] = (low * scale * gains[:, :half]).astype(bf16)
        nbuf[:, half:] = (high * scale * gains[:, half:]).astype(bf16)

        @pl.when(span == 0)
        def _():
            load(0, slot).wait()

        normed = nbuf[...]
        queries = dot(normed, wqkv[slot, :, :hd]).astype(bf16)
        kv[0] = dot(normed, wqkv[slot, :, hd : 2 * hd]).astype(bf16)
        kv[1] = dot(normed, wqkv[slot, :, 2 * hd :]).astype(bf16)

        @pl.when(span == 0)
        def _():
            load(1, slot).wait()

        @pl.when(span == 1)
        def _():
            ag_close(ag2, ag2_in, slot)
            ag_sent(slot)
            update_weights(slot)

        round_weights(slot)

        gate = dot(queries, wb[slot, 0]) * head_scale
        lift = dot(queries, wb[slot, 1]) * head_scale
        hidden = (gate * jax.nn.sigmoid(gate) * lift).astype(bf16)
        answer = dot(hidden, wb[slot, 2], ((1,), (1,))) * head_scale
        answer_mean = jnp.mean(answer * answer, axis=-1, keepdims=True)
        normed_out = (answer * lax.rsqrt(answer_mean + tiny)).astype(bf16)

        @pl.when(span == 0)
        def _():
            load(2, slot).wait()

        for c in range(CHUNKS):
            psend[slot, c] = dot(normed_out, wout[slot, :, c * chunk_cols : (c + 1) * chunk_cols])
            mix(slot, c).start()

        keys = kv[0]
        values = kv[1]
        gate = dot(keys, wb[slot, 0]) * head_scale
        lift = dot(keys, wb[slot, 1]) * head_scale
        up = dot(values, wb[slot, 2]) * (-head_scale)
        logistic = jax.nn.sigmoid(gate)
        act = gate * logistic
        hk_ga_gb[0] = (up * lift * (logistic * (1.0 + gate * (1.0 - logistic)))).astype(bf16)
        hk_ga_gb[1] = (up * act).astype(bf16)
        hk_ga_gb[2] = (act * lift).astype(bf16)

        for c in range(CHUNKS):
            mix(slot, c).wait_recv()
            side, col = c // 2, (c % 2) * chunk_cols
            old = xin[span, side, :, col : col + chunk_cols]
            new = old + (psend[slot, c] + precv[slot, c])
            xin[span, side, :, col : col + chunk_cols] = jnp.where(kept(slot, new.shape), new, old)
        for c in range(CHUNKS):
            mix(slot, c).wait_send()

        @pl.when(slot == 1)
        def _():
            @pl.when(s < sections - 1)
            def _():
                for c in range(CHUNKS):
                    hand_up(span, c).start()

            pltpu.make_async_copy(xin.at[span, h], res.at[span], out_sem.at[span]).start()
            rs1_pass(0)

        for m in range(3):
            rows_m = kv[0] if m < 2 else kv[1]
            sign = head_scale if m < 2 else -head_scale
            for c in range(2):
                part = dot(rows_m, hk_ga_gb[m, :, c * 256 : (c + 1) * 256], ((0,), (0,))) * sign
                for e in range(2):
                    gq[slot, 2 * c + e, m] = part[:, e * 128 : (e + 1) * 128].reshape(
                        gq.shape[3:]
                    )
        rs1_open(slot)

    def one_span(span, carry):
        @pl.when(s == 0)
        def _():
            load_x(span).wait()
            for c in range(CHUNKS):
                share(span, c).start()

        @pl.when(s > 0)
        def _():
            for c in range(CHUNKS):
                hand_up(span, c).wait_recv()
                share(span, c).start()

        for c in range(CHUNKS):
            share_in(span, c).wait_recv()
        for c in range(CHUNKS):
            share(span, c).wait_send()

        def one_slot(slot, inner):
            layer(span, slot)
            return inner

        lax.fori_loop(0, 2, one_slot, 0)

        rs1_close(0)
        rs1_pass(1)
        rs2_pass(0)
        rs2_close(0)

        @pl.when(span == 0)
        def _():
            ag_open(ag1, 0)

        rs1_close(1)

        @pl.when(span == 0)
        def _():
            ag_pass(ag1, ag1_in, 0)

        rs2_pass(1)

        @pl.when(span == 0)
        def _():
            ag_close(ag1, ag1_in, 0)
            ag_open(ag2, 0)

        rs2_close(1)

        @pl.when(span == 0)
        def _():
            ag_open(ag1, 1)
            ag_pass(ag2, ag2_in, 0)
            ag_pass(ag1, ag1_in, 1)
            ag_close(ag1, ag1_in, 1)
            ag_open(ag2, 1)
            ag_pass(ag2, ag2_in, 1)

        rs_sent(0)
        rs_sent(1)
        return carry

    lax.fori_loop(0, 2, one_span, 0)

    def stats(axis, d):
        to = (on_x, on_y)[axis]
        return remote(
            st.at[axis], st_recv.at[axis, d - 1],
            st_send_sem.at[axis, d - 1], st_recv_sem.at[axis, d - 1], to(d),
        )

    for slot in range(2):
        for m in range(3):
            total = jnp.zeros((8, 128), f32)
            for q in range(QUARTERS):
                values = gt[slot, q, m, iy, ix]
                total = total + jnp.sum((values * values).reshape(-1, 8, 128), axis=0)
            st[0, slot * 3 + m] = total
    for axis in range(2):
        for d in (1, 2, 3):
            stats(axis, d).start()
        for d in (1, 2, 3):
            stats(axis, d).wait_recv()
        st[axis + 1] = st[axis] + st_recv[axis, 0] + st_recv[axis, 1] + st_recv[axis, 2]
    for slot in range(2):
        for m in range(3):
            mean = jnp.sum(st[2, slot * 3 + m], keepdims=True) / (hd * hd)
            factor = step_rate * lax.rsqrt(mean + tiny)
            for q in range(QUARTERS):
                old = wfast[slot, m, t, :, q * 128 : (q + 1) * 128]
                new = old - factor * gt[slot, q, m, iy, ix]
                wfast[slot, m, t, :, q * 128 : (q + 1) * 128] = jnp.where(
                    kept(slot, new.shape), new, old
                )
    for slot in range(2):
        for m in range(3):
            pltpu.make_async_copy(
                wfast.at[slot, m, t], fin.at[slot, m], out_sem.at[2 + slot * 3 + m]
            ).start()
    for slot in range(2):
        for m in range(3):
            pltpu.make_async_copy(
                wfast.at[slot, m, t], fin.at[slot, m], out_sem.at[2 + slot * 3 + m]
            ).wait()
    for axis in range(2):
        for d in (1, 2, 3):
            stats(axis, d).wait_send()
    for span in range(2):
        pltpu.make_async_copy(xin.at[span, h], res.at[span], out_sem.at[span]).wait()

        @pl.when(s < sections - 1)
        def _():
            for c in range(CHUNKS):
                hand_up(span, c).wait_send()


def body(stream, counts, norm_gain, w_qkv, w_out, fast_init):
    spans, rows, half = stream.shape
    slots, width, columns = w_qkv.shape[1:]
    hd = fast_init.shape[-1]
    toks = lax.axis_size("tok")
    share = hd // toks
    fast = fast_init.reshape(slots, 3, toks, share, hd)
    gain = norm_gain.reshape(slots, 1, width)
    dma = pltpu.SemaphoreType.DMA
    quarter = hd // QUARTERS
    anywhere = pl.BlockSpec(memory_space=pl.ANY)
    res, fin = pl.pallas_call(
        kernel,
        out_shape=(
            jax.ShapeDtypeStruct((spans, rows, half), f32),
            jax.ShapeDtypeStruct((slots, 3, share, hd), f32),
        ),
        in_specs=[
            anywhere,
            pl.BlockSpec(memory_space=pltpu.SMEM),
            pl.BlockSpec(memory_space=pltpu.VMEM),
            anywhere,
            anywhere,
            anywhere,
        ],
        out_specs=(anywhere, anywhere),
        scratch_shapes=[
            pltpu.VMEM((slots, width, columns), bf16),
            pltpu.VMEM((slots, hd, width), bf16),
            pltpu.VMEM((slots, 3, toks, share, hd), f32),
            pltpu.VMEM((slots, 3, hd, hd), bf16),
            pltpu.VMEM((spans, 2, rows, half), f32),
            pltpu.VMEM((rows, width), bf16),
            pltpu.VMEM((slots, CHUNKS, rows, width // CHUNKS), f32),
            pltpu.VMEM((slots, CHUNKS, rows, width // CHUNKS), f32),
            pltpu.VMEM((2, rows, hd), bf16),
            pltpu.VMEM((3, rows, hd), bf16),
            pltpu.VMEM((slots, QUARTERS, 3, SIDE, SIDE, share, quarter), f32),
            pltpu.VMEM((slots, QUARTERS, 3, SIDE, SIDE, share, quarter), f32),
            pltpu.VMEM((slots, QUARTERS, 3, 3, SIDE, share, quarter), f32),
            pltpu.VMEM((slots, QUARTERS, 3, SIDE, share, quarter), f32),
            pltpu.VMEM((slots, QUARTERS, 3, 3, share, quarter), f32),
            pltpu.VMEM((3, 6, 8, 128), f32),
            pltpu.VMEM((2, 3, 6, 8, 128), f32),
            dma((4, 2)),
            dma((2, CHUNKS)),
            dma((2, CHUNKS)),
            dma((2, CHUNKS)),
            dma((2, CHUNKS)),
            dma((2, CHUNKS)),
            dma((2, CHUNKS)),
        ]
        + [dma((slots, QUARTERS, 3)) for _ in range(8)]
        + [dma((2, 3)), dma((2, 3)), dma((8,))],
        compiler_params=pltpu.CompilerParams(
            collective_id=0, has_side_effects=True, vmem_limit_bytes=67043328
        ),
    )(stream, counts, gain, w_qkv[0], w_out[0], fast)
    return (res[None], fin.reshape(1, slots, 1, 3, share, hd))


def solution(mesh):
    in_specs = (
        P(None, "tok", "head"),
        P(),
        P("segment", None, None),
        P("segment", None, None, "head"),
        P("segment", None, "head", None),
        P("segment", None, "head", None, None, None),
    )
    out_specs = (P("segment", None, "tok", "head"), P("segment", None, "head", None, "tok", None))
    return jax.shard_map(body, mesh=mesh, in_specs=in_specs, out_specs=out_specs, check_vma=False)
```

```python
import contextlib

import jax
import jax.numpy as jnp
from jax import lax
from jax.experimental import pallas as pl
from jax.experimental.pallas import tpu as pltpu
from jax.sharding import PartitionSpec as P

MESH = pl.DeviceIdType.MESH
step_rate = 0.5
tiny = 1e-06
SIDE = 4
QUARTERS = 4
CHUNKS = 2
PIECES = 2
PLAN = (
    "B1", "A3", "C0", "B2", "A4", "C1", "D0", "A5", "B3", "C2", "D1", "E0", "B4", "C3", "D2",
    "E1", "F0", "B5", "C4", "D3", "E2", "F1", "C5", "D4", "E3", "F2", "D5", "E4", "F3", "G0",
    "E5", "F4", "F5",
)

def mark(name):
    return contextlib.nullcontext()


f32 = jnp.float32
bf16 = jnp.bfloat16


def kernel(
    stream, counts, gain, wqkv_hbm, wout_hbm, fast_hbm,
    res, fin,
    wqkv, wout, wfast, wb, xin, nbuf, psend, precv, kv, grads,
    gq, gt, r1, s1, r2, st, st_recv,
    load_sem, x_load, x_send, x_recv, z_send, z_recv, p_send, p_recv,
    rs1_send, rs1_recv, rs2_send, rs2_recv, ag1_send, ag1_recv, ag2_send, ag2_recv,
    st_send_sem, st_recv_sem, res_sem, fin_sem,
):
    sections = lax.axis_size("segment")
    s = lax.axis_index("segment")
    t = lax.axis_index("tok")
    h = lax.axis_index("head")
    iy = t // SIDE
    ix = t % SIDE
    chunk_rows = xin.shape[3]
    half = xin.shape[4]
    width = 2 * half
    piece = chunk_rows // PIECES
    hd = wout.shape[1]
    head_scale = hd ** (-0.5)

    def turn(i, d):
        return (i + d + SIDE) % SIDE

    def on_x(d):
        return {"tok": iy * SIDE + turn(ix, d)}

    def on_y(d):
        return {"tok": turn(iy, d) * SIDE + ix}

    partner = {"head": 1 - h}
    above = {"segment": (s + 1) % sections}
    below = {"segment": (s + sections - 1) % sections}

    def load(kind, slot):
        src, dst = ((wqkv_hbm, wqkv), (fast_hbm, wfast), (wout_hbm, wout))[kind]
        return pltpu.make_async_copy(src.at[slot], dst.at[slot], load_sem.at[kind, slot])

    def load_x(span, c):
        rows = pl.ds(c * chunk_rows, chunk_rows)
        return pltpu.make_async_copy(stream.at[span, rows], xin.at[span, c, h], x_load.at[span, c])

    @pl.when(s == 0)
    def _():
        for span in range(2):
            for c in range(CHUNKS):
                load_x(span, c).start()

    for slot in range(2):
        for kind in range(3):
            load(kind, slot).start()

    barrier = pltpu.get_barrier_semaphore()
    peers = [partner, above, below]
    for d in (1, 2, 3):
        peers += [on_x(d), on_y(d)]
    for peer in peers:
        pl.semaphore_signal(barrier, inc=1, device_id=peer, device_id_type=MESH)
    pl.semaphore_wait(barrier, len(peers))

    def remote(src, dst, send, recv, device):
        return pltpu.make_async_remote_copy(
            src_ref=src, dst_ref=dst, send_sem=send, recv_sem=recv,
            device_id=device, device_id_type=MESH,
        )

    def hand_up(span, c, i):
        part = xin.at[span, c, h, pl.ds(i * piece, piece)]
        return remote(part, part, z_send.at[span, c, i], z_recv.at[span, c, i], above)

    def share(span, c, i):
        part = xin.at[span, c, h, pl.ds(i * piece, piece)]
        return remote(part, part, x_send.at[span, c, i], x_recv.at[span, c, i], partner)

    def share_in(span, c, i):
        part = xin.at[span, c, 1 - h, pl.ds(i * piece, piece)]
        return remote(part, part, x_send.at[span, c, i], x_recv.at[span, c, i], partner)

    def mix(slot, e):
        return remote(
            psend.at[slot, e], precv.at[slot, e], p_send.at[slot, e], p_recv.at[slot, e], partner
        )

    def result(span, c):
        rows = pl.ds(c * chunk_rows, chunk_rows)
        return pltpu.make_async_copy(xin.at[span, c, h], res.at[span, rows], res_sem.at[span, c])

    def order(q):
        forward = 1 if q % 2 == 0 else -1
        if q < 2:
            return forward, iy, on_y, ix, on_x
        return forward, ix, on_x, iy, on_y

    def line(buf, slot, m, q, j):
        return buf.at[slot, m, q, j] if q < 2 else buf.at[slot, m, q, :, j]

    def cell(buf, slot, m, q, j):
        if q < 2:
            return buf.at[slot, m, q, iy, j]
        return buf.at[slot, m, q, j, ix]

    def rs1(slot, m, q, k):
        d, i, to, _, _ = order(q)
        j = (turn(i, 2), turn(i, d), turn(i, -d))[k]
        return remote(
            line(gq, slot, m, q, j), r1.at[slot, m, q, k],
            rs1_send.at[slot, m, q, k], rs1_recv.at[slot, m, q, k], to(d if k < 2 else -d),
        )

    def rs2(slot, m, q, k):
        _, _, _, i, to = order(q)
        return remote(
            s1.at[slot, m, q, turn(i, k + 1)], r2.at[slot, m, q, k],
            rs2_send.at[slot, m, q, k], rs2_recv.at[slot, m, q, k], to(k + 1),
        )

    def ag1(slot, m, q, k):
        _, _, _, i, to = order(q)
        part = cell(gt, slot, m, q, i)
        return remote(
            part, part, ag1_send.at[slot, m, q, k], ag1_recv.at[slot, m, q, k], to(k + 1)
        )

    def ag1_in(slot, m, q, k):
        _, _, _, i, to = order(q)
        part = cell(gt, slot, m, q, turn(i, -(k + 1)))
        return remote(
            part, part, ag1_send.at[slot, m, q, k], ag1_recv.at[slot, m, q, k], to(k + 1)
        )

    def ag2(slot, m, q, k):
        d, i, to, _, _ = order(q)
        part = line(gt, slot, m, q, (i, i, turn(i, -d))[k])
        return remote(
            part, part, ag2_send.at[slot, m, q, k], ag2_recv.at[slot, m, q, k], to((d, -d, d)[k])
        )

    def ag2_in(slot, m, q, k):
        d, i, to, _, _ = order(q)
        part = line(gt, slot, m, q, (turn(i, -d), turn(i, d), turn(i, 2))[k])
        return remote(
            part, part, ag2_send.at[slot, m, q, k], ag2_recv.at[slot, m, q, k], to((d, -d, d)[k])
        )

    def rs1_open(slot, m):
        for k in (0, 2):
            for q in range(QUARTERS):
                rs1(slot, m, q, k).start()

    def rs1_pass(slot, m):
        for q in range(QUARTERS):
            d, i, _, _, _ = order(q)
            rs1(slot, m, q, 0).wait_recv()
            block = line(gq, slot, m, q, turn(i, d))
            block[...] = block[...] + r1[slot, m, q, 0]
            rs1(slot, m, q, 1).start()

    def rs1_close(slot, m):
        for q in range(QUARTERS):
            _, i, _, _, _ = order(q)
            rs1(slot, m, q, 2).wait_recv()
            rs1(slot, m, q, 1).wait_recv()
            s1[slot, m, q] = line(gq, slot, m, q, i)[...] + r1[slot, m, q, 1] + r1[slot, m, q, 2]
            for k in range(3):
                rs2(slot, m, q, k).start()

    def rs2_close(slot, m):
        for q in range(QUARTERS):
            _, _, _, i, _ = order(q)
            for k in range(3):
                rs2(slot, m, q, k).wait_recv()
            cell(gt, slot, m, q, i)[...] = (
                s1[slot, m, q, i] + r2[slot, m, q, 0] + (r2[slot, m, q, 1] + r2[slot, m, q, 2])
            )

    def ag1_open(slot, m):
        for q in range(QUARTERS):
            for k in range(3):
                ag1(slot, m, q, k).start()

    def ag2_open(slot, m):
        for q in range(QUARTERS):
            for k in range(3):
                ag1_in(slot, m, q, k).wait_recv()
            ag2(slot, m, q, 0).start()
            ag2(slot, m, q, 1).start()

    def ag2_pass(slot, m):
        for q in range(QUARTERS):
            ag2_in(slot, m, q, 0).wait_recv()
            ag2(slot, m, q, 2).start()

    def ag2_close(slot, m):
        for q in range(QUARTERS):
            ag2_in(slot, m, q, 1).wait_recv()
            ag2_in(slot, m, q, 2).wait_recv()

    def rs_sent(slot, m):
        for q in range(QUARTERS):
            for k in range(3):
                rs1(slot, m, q, k).wait_send()
                rs2(slot, m, q, k).wait_send()

    def ag_sent(slot, m):
        for q in range(QUARTERS):
            for k in range(3):
                ag1(slot, m, q, k).wait_send()
                ag2(slot, m, q, k).wait_send()

    def kept(slot, shape):
        return jnp.broadcast_to(counts[s], shape) > slot

    def update_weights(slot, m):
        def squares(b, total):
            part = total
            for q in range(QUARTERS):
                values = gt[slot, m, q, b]
                part = part + jnp.sum(values * values, axis=0)
            return part

        total = lax.fori_loop(0, SIDE, squares, jnp.zeros(gt.shape[-2:], f32))
        mean = jnp.sum(total, keepdims=True) / (hd * hd)
        factor = step_rate * lax.rsqrt(mean + tiny)

        def change(b, carry):
            for q in range(QUARTERS):
                cols = pl.ds(q * 128, 128)
                old = wfast[slot, m, pl.ds(b * SIDE, SIDE), :, cols]
                new = old - factor * gt[slot, m, q, b]
                new = jnp.where(kept(slot, new.shape), new, old)
                wfast[slot, m, pl.ds(b * SIDE, SIDE), :, cols] = new
                height = SIDE * new.shape[1]
                wb[slot, m, pl.ds(b * height, height), cols] = new.reshape(height, -1).astype(bf16)
            return carry

        lax.fori_loop(0, SIDE, change, 0)

    def round_weights(slot):
        for m in range(3):

            def one(b, carry):
                block = wfast[slot, m, pl.ds(b * SIDE, SIDE)]
                height = SIDE * block.shape[1]
                wb[slot, m, pl.ds(b * height, height)] = block.reshape(height, hd).astype(bf16)
                return carry

            lax.fori_loop(0, SIDE, one, 0)

    def finish_weights(slot):
        for m in range(3):
            ag2_close(slot, m)
            update_weights(slot, m)
        for m in range(3):
            ag_sent(slot, m)

    def dot(a, b, dims=((1,), (0,))):
        return lax.dot_general(a, b, (dims, ((), ())), preferred_element_type=f32)

    def layer(span, c, slot):
        first = (span == 0) & (c == 0)

        with mark("norm"):
            low = xin[span, c, 0]
            high = xin[span, c, 1]
            mean = (
                jnp.sum(low * low, axis=-1, keepdims=True)
                + jnp.sum(high * high, axis=-1, keepdims=True)
            ) / width
            scale = lax.rsqrt(mean + tiny)
            gains = gain[pl.ds(slot, 1), :]
            nbuf[:, :half] = (low * scale * gains[:, :half]).astype(bf16)
            nbuf[:, half:] = (high * scale * gains[:, half:]).astype(bf16)

        @pl.when(first)
        def _():
            load(0, slot).wait()

        with mark("qkv"):
            normed = nbuf[...]
            queries = dot(normed, wqkv[slot, :, :hd]).astype(bf16)
            kv[slot, 0, c] = dot(normed, wqkv[slot, :, hd : 2 * hd]).astype(bf16)
            kv[slot, 1, c] = dot(normed, wqkv[slot, :, 2 * hd :]).astype(bf16)

        @pl.when(first)
        def _():
            load(1, slot).wait()
            with mark("round"):
                round_weights(slot)
            load(2, slot).wait()

        @pl.when((span == 1) & (c == 0) & (slot == 1))
        def _():
            with mark("finish1"):
                finish_weights(1)

        with mark("qmap"):
            gate = dot(queries, wb[slot, 0]) * head_scale
            lift = dot(queries, wb[slot, 1]) * head_scale
            hidden = (gate * jax.nn.sigmoid(gate) * lift).astype(bf16)
            answer = dot(hidden, wb[slot, 2], ((1,), (1,))) * head_scale
            answer_mean = jnp.mean(answer * answer, axis=-1, keepdims=True)
            normed_out = (answer * lax.rsqrt(answer_mean + tiny)).astype(bf16)

        with mark("outp"):
            for e in range(2):
                psend[slot, e] = dot(normed_out, wout[slot, :, e * half : (e + 1) * half])
                mix(slot, e).start()

        with mark("kvpath"):
            keys = kv[slot, 0, c]
            values = kv[slot, 1, c]
            gate = dot(keys, wb[slot, 0]) * head_scale
            lift = dot(keys, wb[slot, 1]) * head_scale
            up = dot(values, wb[slot, 2]) * (-head_scale)
            logistic = jax.nn.sigmoid(gate)
            act = gate * logistic
            grads[slot, 0, c] = (
                up * lift * (logistic * (1.0 + gate * (1.0 - logistic)))
            ).astype(bf16)
            grads[slot, 1, c] = (up * act).astype(bf16)
            grads[slot, 2, c] = (act * lift).astype(bf16)

        with mark("mixwait"):
            for e in range(2):
                mix(slot, e).wait_recv()
                old = xin[span, c, e]
                new = old + (psend[slot, e] + precv[slot, e])
                xin[span, c, e] = jnp.where(kept(slot, new.shape), new, old)
            for e in range(2):
                mix(slot, e).wait_send()

        @pl.when(slot == 1)
        def _():
            @pl.when(s < sections - 1)
            def _():
                for i in range(PIECES):
                    hand_up(span, c, i).start()

            result(span, c).start()

        @pl.when(c == CHUNKS - 1)
        def _():
            @pl.when(slot == 1)
            def _():
                with mark("B0"):
                    rs1_pass(0, 0)

            with mark("gdots"):
                for m in range(3):
                    terms = kv[slot, 0 if m < 2 else 1].reshape(-1, hd)
                    sign = head_scale if m < 2 else -head_scale
                    for e in range(2):
                        cols = grads[slot, m, :, :, e * 256 : (e + 1) * 256].reshape(-1, 256)
                        part = dot(terms, cols, ((0,), (0,))) * sign
                        for f in range(2):
                            gq[slot, m, 2 * e + f] = part[:, f * 128 : (f + 1) * 128].reshape(
                                gq.shape[3:]
                            )

                    @pl.when(slot == 0)
                    def _():
                        rs1_open(slot, m)

    @pl.when(s == 0)
    def _():
        for span in range(2):
            for c in range(CHUNKS):
                load_x(span, c).wait()
                for i in range(PIECES):
                    share(span, c, i).start()

    def run_plan(span):
        def stage(name, unit):
            slot, m = unit // 3, unit % 3
            only_first = {"D": ag1_open, "E": ag2_open, "F": ag2_pass}
            always = {"A": rs1_open, "B": rs1_pass, "C": rs1_close, "D": rs2_close}
            with mark(name + str(unit)):
                if name in always:
                    always[name](slot, m)
                if name in only_first:

                    @pl.when(span == 0)
                    def _():
                        only_first[name](slot, m)

                if name == "G":

                    @pl.when(span == 0)
                    def _():
                        finish_weights(0)

        for step in PLAN:
            stage(step[0], int(step[1]))

    def one_span(span, carry):
        def one_chunk(c, inner):
            @pl.when(s > 0)
            def _():
                for i in range(PIECES):
                    with mark("hand"):
                        hand_up(span, c, i).wait_recv()
                    share(span, c, i).start()

            with mark("share"):
                for i in range(PIECES):
                    share_in(span, c, i).wait_recv()
                for i in range(PIECES):
                    share(span, c, i).wait_send()

            def one_slot(slot, innermost):
                layer(span, c, slot)
                return innermost

            lax.fori_loop(0, 2, one_slot, 0)
            return inner

        lax.fori_loop(0, CHUNKS, one_chunk, 0)
        run_plan(span)
        with mark("sent"):
            for unit in range(6):
                rs_sent(unit // 3, unit % 3)
        return carry

    lax.fori_loop(0, 2, one_span, 0)

    def stats(axis, d):
        to = (on_x, on_y)[axis]
        return remote(
            st.at[axis], st_recv.at[axis, d - 1],
            st_send_sem.at[axis, d - 1], st_recv_sem.at[axis, d - 1], to(d),
        )

    for slot in range(2):
        for m in range(3):
            total = jnp.zeros((8, 128), f32)
            for q in range(QUARTERS):
                values = gt[slot, m, q, iy, ix]
                total = total + jnp.sum((values * values).reshape(-1, 8, 128), axis=0)
            st[0, slot * 3 + m] = total
    for axis in range(2):
        for d in (1, 2, 3):
            stats(axis, d).start()
        with mark("stats"):
            for d in (1, 2, 3):
                stats(axis, d).wait_recv()
        st[axis + 1] = st[axis] + st_recv[axis, 0] + st_recv[axis, 1] + st_recv[axis, 2]

    def final(slot, m):
        return pltpu.make_async_copy(wfast.at[slot, m, t], fin.at[slot, m], fin_sem.at[slot, m])

    for slot in range(2):
        for m in range(3):
            mean = jnp.sum(st[2, slot * 3 + m], keepdims=True) / (hd * hd)
            factor = step_rate * lax.rsqrt(mean + tiny)
            for q in range(QUARTERS):
                old = wfast[slot, m, t, :, q * 128 : (q + 1) * 128]
                new = old - factor * gt[slot, m, q, iy, ix]
                wfast[slot, m, t, :, q * 128 : (q + 1) * 128] = jnp.where(
                    kept(slot, new.shape), new, old
                )
            final(slot, m).start()
    for slot in range(2):
        for m in range(3):
            final(slot, m).wait()
    for axis in range(2):
        for d in (1, 2, 3):
            stats(axis, d).wait_send()
    for span in range(2):
        for c in range(CHUNKS):
            result(span, c).wait()

            @pl.when(s < sections - 1)
            def _():
                for i in range(PIECES):
                    hand_up(span, c, i).wait_send()


def body(stream, counts, norm_gain, w_qkv, w_out, fast_init):
    spans, rows, half = stream.shape
    slots, width, columns = w_qkv.shape[1:]
    hd = fast_init.shape[-1]
    toks = lax.axis_size("tok")
    share = hd // toks
    fast = fast_init.reshape(slots, 3, toks, share, hd)
    part = rows // CHUNKS
    dma = pltpu.SemaphoreType.DMA
    quarter = hd // QUARTERS
    anywhere = pl.BlockSpec(memory_space=pl.ANY)
    res, fin = pl.pallas_call(
        kernel,
        out_shape=(
            jax.ShapeDtypeStruct((spans, rows, half), f32),
            jax.ShapeDtypeStruct((slots, 3, share, hd), f32),
        ),
        in_specs=[
            anywhere,
            pl.BlockSpec(memory_space=pltpu.SMEM),
            pl.BlockSpec(memory_space=pltpu.VMEM),
            anywhere,
            anywhere,
            anywhere,
        ],
        out_specs=(anywhere, anywhere),
        scratch_shapes=[
            pltpu.VMEM((slots, width, columns), bf16),
            pltpu.VMEM((slots, hd, width), bf16),
            pltpu.VMEM((slots, 3, toks, share, hd), f32),
            pltpu.VMEM((slots, 3, hd, hd), bf16),
            pltpu.VMEM((spans, CHUNKS, 2, part, half), f32),
            pltpu.VMEM((part, width), bf16),
            pltpu.VMEM((2, 2, part, half), f32),
            pltpu.VMEM((2, 2, part, half), f32),
            pltpu.VMEM((slots, 2, CHUNKS, part, hd), bf16),
            pltpu.VMEM((slots, 3, CHUNKS, part, hd), bf16),
            pltpu.VMEM((slots, 3, QUARTERS, SIDE, SIDE, share, quarter), f32),
            pltpu.VMEM((slots, 3, QUARTERS, SIDE, SIDE, share, quarter), f32),
            pltpu.VMEM((slots, 3, QUARTERS, 3, SIDE, share, quarter), f32),
            pltpu.VMEM((slots, 3, QUARTERS, SIDE, share, quarter), f32),
            pltpu.VMEM((slots, 3, QUARTERS, 3, share, quarter), f32),
            pltpu.VMEM((3, 6, 8, 128), f32),
            pltpu.VMEM((2, 3, 6, 8, 128), f32),
            dma((3, slots)),
            dma((spans, CHUNKS)),
        ]
        + [dma((spans, CHUNKS, PIECES)) for _ in range(4)]
        + [dma((2, 2)) for _ in range(2)]
        + [dma((slots, 3, QUARTERS, 3)) for _ in range(8)]
        + [dma((2, 3)), dma((2, 3)), dma((spans, CHUNKS)), dma((slots, 3))],
        compiler_params=pltpu.CompilerParams(
            collective_id=0, has_side_effects=True, vmem_limit_bytes=67043328
        ),
    )(stream, counts, norm_gain[0], w_qkv[0], w_out[0], fast)
    return (res[None], fin.reshape(1, slots, 1, 3, share, hd))


def solution(mesh):
    in_specs = (
        P(None, "tok", "head"),
        P(),
        P("segment", None, None),
        P("segment", None, None, "head"),
        P("segment", None, "head", None),
        P("segment", None, "head", None, None, None),
    )
    out_specs = (P("segment", None, "tok", "head"), P("segment", None, "head", None, "tok", None))
    return jax.shard_map(body, mesh=mesh, in_specs=in_specs, out_specs=out_specs, check_vma=False)
```

```python
import contextlib
import functools

import jax
import jax.numpy as jnp
from jax import lax
from jax.experimental import pallas as pl
from jax.experimental.pallas import tpu as pltpu
from jax.sharding import PartitionSpec as P

MESH = pl.DeviceIdType.MESH
step_rate = 0.5
tiny = 1e-06
SIDE = 4
QUARTERS = 4
PIECES = 4
PLAN_TWO = (
    "B0", "A3", "B1", "A4", "C0", "B2", "A5", "C1", "D0", "B3", "C2", "D1", "E0", "B4", "C3",
    "D2", "E1", "F0", "B5", "C4", "D3", "E2", "F1", "C5", "D4", "E3", "F2", "D5", "E4", "F3",
    "H0", "H1", "H2", "E5", "F4", "H3", "F5",
)
PLAN_ONE = (
    "B0", "B1", "C0", "B2", "C1", "D0", "C2", "D1", "E0", "D2", "E1", "F0", "E2", "F1", "H0",
    "F2", "H1", "H2",
)


def mark(name):
    return contextlib.nullcontext()


f32 = jnp.float32
bf16 = jnp.bfloat16


def on(condition, run):
    if condition is True:
        run()
    elif condition is not False:
        pl.when(condition)(run)


def kernel(
    deep,
    stream, counts, gain, wqkv_hbm, wout_hbm, fast_hbm,
    res, fin,
    wqkv, wout, wfast, wb, xin, acc, squares, psend, precv, kv, grads,
    gq, gt, r1, s1, r2, st, st_recv,
    load_sem, x_load, x_send, x_recv, z_send, z_recv, p_send, p_recv,
    rs1_send, rs1_recv, rs2_send, rs2_recv, ag1_send, ag1_recv, ag2_send, ag2_recv,
    st_send_sem, st_recv_sem, res_sem, fin_sem,
):
    sections = lax.axis_size("segment")
    s = lax.axis_index("segment")
    t = lax.axis_index("tok")
    h = lax.axis_index("head")
    iy = t // SIDE
    ix = t % SIDE
    piece = xin.shape[4]
    half = piece * PIECES
    width = 2 * half
    hd = wout.shape[1]
    head_scale = hd ** (-0.5)

    def turn(i, d):
        return (i + d + SIDE) % SIDE

    def on_x(d):
        return {"tok": iy * SIDE + turn(ix, d)}

    def on_y(d):
        return {"tok": turn(iy, d) * SIDE + ix}

    partner = {"head": 1 - h}
    above = {"segment": (s + 1) % sections}
    below = {"segment": (s + sections - 1) % sections}

    def load(kind, slot):
        src, dst = ((wqkv_hbm, wqkv), (fast_hbm, wfast), (wout_hbm, wout))[kind]
        return pltpu.make_async_copy(src.at[slot], dst.at[slot], load_sem.at[kind, slot])

    def cols(p, side=0):
        return pl.ds(side * half + p * piece, piece)

    def load_x(span, p):
        return pltpu.make_async_copy(
            stream.at[span, :, cols(p)], xin.at[span, p, h], x_load.at[span, p]
        )

    @pl.when(s == 0)
    def _():
        for span in range(2):
            for p in range(PIECES):
                load_x(span, p).start()

    for slot in range(2):
        for kind in range(3):
            load(kind, slot).start()

    barrier = pltpu.get_barrier_semaphore()
    peers = [partner, above, below]
    for d in (1, 2, 3):
        peers += [on_x(d), on_y(d)]
    for peer in peers:
        pl.semaphore_signal(barrier, inc=1, device_id=peer, device_id_type=MESH)
    pl.semaphore_wait(barrier, len(peers))

    def remote(src, dst, send, recv, device):
        return pltpu.make_async_remote_copy(
            src_ref=src, dst_ref=dst, send_sem=send, recv_sem=recv,
            device_id=device, device_id_type=MESH,
        )

    def hand_up(span, p):
        part = xin.at[span, p, h]
        return remote(part, part, z_send.at[span, p], z_recv.at[span, p], above)

    def share(span, p):
        part = xin.at[span, p, h]
        return remote(part, part, x_send.at[span, p], x_recv.at[span, p], partner)

    def share_in(span, p):
        part = xin.at[span, p, 1 - h]
        return remote(part, part, x_send.at[span, p], x_recv.at[span, p], partner)

    def mix(slot, p):
        return remote(
            psend.at[slot, p], precv.at[slot, p], p_send.at[slot, p], p_recv.at[slot, p], partner
        )

    def result(span, p):
        return pltpu.make_async_copy(
            xin.at[span, p, h], res.at[span, :, cols(p)], res_sem.at[span, p]
        )

    def order(q):
        forward = 1 if q % 2 == 0 else -1
        if q < 2:
            return forward, iy, on_y, ix, on_x
        return forward, ix, on_x, iy, on_y

    def line(buf, slot, m, q, j):
        return buf.at[slot, m, q, j] if q < 2 else buf.at[slot, m, q, :, j]

    def cell(buf, slot, m, q, j):
        if q < 2:
            return buf.at[slot, m, q, iy, j]
        return buf.at[slot, m, q, j, ix]

    def rs1(slot, m, q, k):
        d, i, to, _, _ = order(q)
        j = (turn(i, 2), turn(i, d), turn(i, -d))[k]
        return remote(
            line(gq, slot, m, q, j), r1.at[slot, m, q, k],
            rs1_send.at[slot, m, q, k], rs1_recv.at[slot, m, q, k], to(d if k < 2 else -d),
        )

    def rs2(slot, m, q, k):
        _, _, _, i, to = order(q)
        return remote(
            s1.at[slot, m, q, turn(i, k + 1)], r2.at[slot, m, q, k],
            rs2_send.at[slot, m, q, k], rs2_recv.at[slot, m, q, k], to(k + 1),
        )

    def ag1(slot, m, q, k):
        _, _, _, i, to = order(q)
        part = cell(gt, slot, m, q, i)
        return remote(
            part, part, ag1_send.at[slot, m, q, k], ag1_recv.at[slot, m, q, k], to(k + 1)
        )

    def ag1_in(slot, m, q, k):
        _, _, _, i, to = order(q)
        part = cell(gt, slot, m, q, turn(i, -(k + 1)))
        return remote(
            part, part, ag1_send.at[slot, m, q, k], ag1_recv.at[slot, m, q, k], to(k + 1)
        )

    def ag2(slot, m, q, k):
        d, i, to, _, _ = order(q)
        part = line(gt, slot, m, q, (i, i, turn(i, -d))[k])
        return remote(
            part, part, ag2_send.at[slot, m, q, k], ag2_recv.at[slot, m, q, k], to((d, -d, d)[k])
        )

    def ag2_in(slot, m, q, k):
        d, i, to, _, _ = order(q)
        part = line(gt, slot, m, q, (turn(i, -d), turn(i, d), turn(i, 2))[k])
        return remote(
            part, part, ag2_send.at[slot, m, q, k], ag2_recv.at[slot, m, q, k], to((d, -d, d)[k])
        )

    def rs1_open(slot, m):
        for k in (0, 2):
            for q in range(QUARTERS):
                rs1(slot, m, q, k).start()

    def rs1_pass(slot, m):
        for q in range(QUARTERS):
            d, i, _, _, _ = order(q)
            rs1(slot, m, q, 0).wait_recv()
            block = line(gq, slot, m, q, turn(i, d))
            block[...] = block[...] + r1[slot, m, q, 0]
            rs1(slot, m, q, 1).start()

    def rs1_close(slot, m):
        for q in range(QUARTERS):
            _, i, _, _, _ = order(q)
            rs1(slot, m, q, 2).wait_recv()
            rs1(slot, m, q, 1).wait_recv()
            s1[slot, m, q] = line(gq, slot, m, q, i)[...] + r1[slot, m, q, 1] + r1[slot, m, q, 2]
            for k in range(3):
                rs2(slot, m, q, k).start()

    def rs2_close(slot, m):
        for q in range(QUARTERS):
            _, _, _, i, _ = order(q)
            for k in range(3):
                rs2(slot, m, q, k).wait_recv()
            cell(gt, slot, m, q, i)[...] = (
                s1[slot, m, q, i] + r2[slot, m, q, 0] + (r2[slot, m, q, 1] + r2[slot, m, q, 2])
            )

    def ag1_open(slot, m):
        for q in range(QUARTERS):
            for k in range(3):
                ag1(slot, m, q, k).start()

    def ag2_open(slot, m):
        for q in range(QUARTERS):
            for k in range(3):
                ag1_in(slot, m, q, k).wait_recv()
            ag2(slot, m, q, 0).start()
            ag2(slot, m, q, 1).start()

    def ag2_pass(slot, m):
        for q in range(QUARTERS):
            ag2_in(slot, m, q, 0).wait_recv()
            ag2(slot, m, q, 2).start()

    def ag2_close(slot, m):
        for q in range(QUARTERS):
            ag2_in(slot, m, q, 1).wait_recv()
            ag2_in(slot, m, q, 2).wait_recv()

    def rs_sent(slot, m):
        for q in range(QUARTERS):
            for k in range(3):
                rs1(slot, m, q, k).wait_send()
                rs2(slot, m, q, k).wait_send()

    def ag_sent(slot, m):
        for q in range(QUARTERS):
            for k in range(3):
                ag1(slot, m, q, k).wait_send()
                ag2(slot, m, q, k).wait_send()

    def kept(slot, shape):
        return jnp.broadcast_to(counts[s], shape) > slot

    def update_weights(slot, m):
        def add_squares(b, total):
            part = total
            for q in range(QUARTERS):
                values = gt[slot, m, q, b]
                part = part + jnp.sum(values * values, axis=0)
            return part

        total = lax.fori_loop(0, SIDE, add_squares, jnp.zeros(gt.shape[-2:], f32))
        mean = jnp.sum(total, keepdims=True) / (hd * hd)
        factor = step_rate * lax.rsqrt(mean + tiny)

        def change(b, carry):
            for q in range(QUARTERS):
                lanes = pl.ds(q * 128, 128)
                old = wfast[slot, m, pl.ds(b * SIDE, SIDE), :, lanes]
                new = old - factor * gt[slot, m, q, b]
                new = jnp.where(kept(slot, new.shape), new, old)
                wfast[slot, m, pl.ds(b * SIDE, SIDE), :, lanes] = new
                height = SIDE * new.shape[1]
                wb[slot, m, pl.ds(b * height, height), lanes] = new.reshape(height, -1).astype(bf16)
            return carry

        lax.fori_loop(0, SIDE, change, 0)

    def round_weights(slot):
        for m in range(3):

            def one(b, carry):
                block = wfast[slot, m, pl.ds(b * SIDE, SIDE)]
                height = SIDE * block.shape[1]
                wb[slot, m, pl.ds(b * height, height)] = block.reshape(height, hd).astype(bf16)
                return carry

            lax.fori_loop(0, SIDE, one, 0)

    def finish_weights(slot, m):
        ag2_close(slot, m)
        update_weights(slot, m)
        ag_sent(slot, m)

    def dot(a, b, dims=((1,), (0,))):
        return lax.dot_general(a, b, (dims, ((), ())), preferred_element_type=f32)

    two = True if all(deep) else sum((s == i).astype(jnp.int32) for i, d in enumerate(deep) if d) > 0
    one = False if two is True else jnp.logical_not(two)

    def qkv_piece(span, slot, p):
        low = xin[span, p, 0]
        high = xin[span, p, 1]
        both = low * low + high * high
        low = (low * gain[slot : slot + 1, cols(p)]).astype(bf16)
        high = (high * gain[slot : slot + 1, cols(p, 1)]).astype(bf16)
        terms = dot(low, wqkv[slot, cols(p)]) + dot(high, wqkv[slot, cols(p, 1)])
        squares[...] = both if p == 0 else squares[...] + both
        acc[...] = terms if p == 0 else acc[...] + terms

    def arrive(span):
        for p in range(PIECES):

            @pl.when(s == 0)
            def _():
                load_x(span, p).wait()

            @pl.when(s > 0)
            def _():
                with mark("hand"):
                    hand_up(span, p).wait_recv()

            share(span, p).start()
            with mark("share"):
                share_in(span, p).wait_recv()
            if p == 0:

                @pl.when(span == 0)
                def _():
                    load(0, 0).wait()

            with mark("qkv"):
                qkv_piece(span, 0, p)
        for p in range(PIECES):
            share(span, p).wait_send()

    def layer(span, slot):
        mean = jnp.sum(squares[...], axis=-1, keepdims=True) / width
        scale = lax.rsqrt(mean + tiny)
        queries = (acc[:, :hd] * scale).astype(bf16)
        kv[slot, 0] = (acc[:, hd : 2 * hd] * scale).astype(bf16)
        kv[slot, 1] = (acc[:, 2 * hd :] * scale).astype(bf16)

        @pl.when(span == 0)
        def _():
            load(1, slot).wait()
            with mark("round"):
                round_weights(slot)
            load(2, slot).wait()

        if slot == 1:

            @pl.when(span == 1)
            def _():
                with mark("finish1"):
                    finish_weights(1, 1)
                    finish_weights(1, 2)

        with mark("qmap"):
            gate = dot(queries, wb[slot, 0]) * head_scale
            lift = dot(queries, wb[slot, 1]) * head_scale
            hidden = (gate * jax.nn.sigmoid(gate) * lift).astype(bf16)
            answer = dot(hidden, wb[slot, 2], ((1,), (1,))) * head_scale
            answer_mean = jnp.mean(answer * answer, axis=-1, keepdims=True)
            normed_out = (answer * lax.rsqrt(answer_mean + tiny)).astype(bf16)

        with mark("outp"):
            for p in range(PIECES):
                for side in range(2):
                    psend[slot, p, side] = dot(normed_out, wout[slot, :, cols(p, side)])
                if p % 2 == 1:
                    mix(slot, p - 1).start()
                    mix(slot, p).start()

        with mark("kvpath"):
            keys = kv[slot, 0]
            values = kv[slot, 1]
            gate = dot(keys, wb[slot, 0]) * head_scale
            lift = dot(keys, wb[slot, 1]) * head_scale
            up = dot(values, wb[slot, 2]) * (-head_scale)
            logistic = jax.nn.sigmoid(gate)
            act = gate * logistic
            grads[0] = (up * lift * (logistic * (1.0 + gate * (1.0 - logistic)))).astype(bf16)
            grads[1] = (up * act).astype(bf16)
            grads[2] = (act * lift).astype(bf16)

        with mark("gdots"):
            for m in range(3):
                terms = kv[slot, 0 if m < 2 else 1]
                sign = head_scale if m < 2 else -head_scale
                for e in range(2):
                    part = dot(terms, grads[m, :, e * 256 : (e + 1) * 256], ((0,), (0,))) * sign
                    for f in range(2):
                        gq[slot, m, 2 * e + f] = part[:, f * 128 : (f + 1) * 128].reshape(
                            gq.shape[3:]
                        )
        if slot == 0:
            for m in range(3):
                rs1_open(slot, m)

        if slot == 0:

            @pl.when(span == 0)
            def _():
                load(0, 1).wait()

        for p in range(PIECES):
            with mark("mixwait"):
                mix(slot, p).wait_recv()
            old = xin[span, p]
            new = old + (psend[slot, p] + precv[slot, p])
            xin[span, p] = jnp.where(kept(slot, new.shape), new, old)

            def leave():
                @pl.when(s < sections - 1)
                def _():
                    hand_up(span, p).start()

                result(span, p).start()

            def go_on():
                with mark("qkv"):
                    qkv_piece(span, 1, p)

            if slot == 0:
                on(two, go_on)
                on(one, leave)
            else:
                leave()
        for p in range(PIECES):
            mix(slot, p).wait_send()

    def run_plan(span, plan):
        def stage(name, unit):
            slot, m = unit // 3, unit % 3
            only_first = {"D": ag1_open, "E": ag2_open, "F": ag2_pass, "H": finish_weights}
            always = {"A": rs1_open, "B": rs1_pass, "C": rs1_close, "D": rs2_close}
            with mark(name + str(unit)):
                if name in always:
                    always[name](slot, m)
                if name in only_first:

                    @pl.when(span == 0)
                    def _():
                        only_first[name](slot, m)

        for step in plan:
            stage(step[0], int(step[1]))
        for unit in range(6 if plan is PLAN_TWO else 3):
            rs_sent(unit // 3, unit % 3)

    def one_span(span, carry):
        arrive(span)
        layer(span, 0)

        def rest_two():
            layer(span, 1)
            run_plan(span, PLAN_TWO)

        on(two, rest_two)
        on(one, lambda: run_plan(span, PLAN_ONE))
        return carry

    lax.fori_loop(0, 2, one_span, 0)

    if two is not True:

        @pl.when(one)
        def _():
            load(1, 1).wait()
            load(2, 1).wait()

    def stats(axis, d):
        to = (on_x, on_y)[axis]
        return remote(
            st.at[axis], st_recv.at[axis, d - 1],
            st_send_sem.at[axis, d - 1], st_recv_sem.at[axis, d - 1], to(d),
        )

    def own_squares(slot):
        for m in range(3):
            total = jnp.zeros((8, 128), f32)
            for q in range(QUARTERS):
                values = gt[slot, m, q, iy, ix]
                total = total + jnp.sum((values * values).reshape(-1, 8, 128), axis=0)
            st[0, slot * 3 + m] = total

    own_squares(0)
    on(two, lambda: own_squares(1))
    for axis in range(2):
        for d in (1, 2, 3):
            stats(axis, d).start()
        with mark("stats"):
            for d in (1, 2, 3):
                stats(axis, d).wait_recv()
        st[axis + 1] = st[axis] + st_recv[axis, 0] + st_recv[axis, 1] + st_recv[axis, 2]

    def final(slot, m):
        return pltpu.make_async_copy(wfast.at[slot, m, t], fin.at[slot, m], fin_sem.at[slot, m])

    def last_update(slot):
        for m in range(3):
            mean = jnp.sum(st[2, slot * 3 + m], keepdims=True) / (hd * hd)
            factor = step_rate * lax.rsqrt(mean + tiny)
            for q in range(QUARTERS):
                old = wfast[slot, m, t, :, q * 128 : (q + 1) * 128]
                new = old - factor * gt[slot, m, q, iy, ix]
                wfast[slot, m, t, :, q * 128 : (q + 1) * 128] = jnp.where(
                    kept(slot, new.shape), new, old
                )

    last_update(0)
    on(two, lambda: last_update(1))
    for slot in range(2):
        for m in range(3):
            final(slot, m).start()
    for slot in range(2):
        for m in range(3):
            final(slot, m).wait()
    for axis in range(2):
        for d in (1, 2, 3):
            stats(axis, d).wait_send()
    for span in range(2):
        for p in range(PIECES):
            result(span, p).wait()

            @pl.when(s < sections - 1)
            def _():
                hand_up(span, p).wait_send()


def body(stream, counts, norm_gain, w_qkv, w_out, fast_init):
    spans, rows, half = stream.shape
    slots, width, columns = w_qkv.shape[1:]
    hd = fast_init.shape[-1]
    toks = lax.axis_size("tok")
    share = hd // toks
    fast = fast_init.reshape(slots, 3, toks, share, hd)
    piece = half // PIECES
    deep = (True,) * lax.axis_size("segment")
    dma = pltpu.SemaphoreType.DMA
    quarter = hd // QUARTERS
    anywhere = pl.BlockSpec(memory_space=pl.ANY)
    res, fin = pl.pallas_call(
        functools.partial(kernel, deep),
        out_shape=(
            jax.ShapeDtypeStruct((spans, rows, half), f32),
            jax.ShapeDtypeStruct((slots, 3, share, hd), f32),
        ),
        in_specs=[
            anywhere,
            pl.BlockSpec(memory_space=pltpu.SMEM),
            pl.BlockSpec(memory_space=pltpu.VMEM),
            anywhere,
            anywhere,
            anywhere,
        ],
        out_specs=(anywhere, anywhere),
        scratch_shapes=[
            pltpu.VMEM((slots, width, columns), bf16),
            pltpu.VMEM((slots, hd, width), bf16),
            pltpu.VMEM((slots, 3, toks, share, hd), f32),
            pltpu.VMEM((slots, 3, hd, hd), bf16),
            pltpu.VMEM((spans, PIECES, 2, rows, piece), f32),
            pltpu.VMEM((rows, columns), f32),
            pltpu.VMEM((rows, piece), f32),
            pltpu.VMEM((slots, PIECES, 2, rows, piece), f32),
            pltpu.VMEM((slots, PIECES, 2, rows, piece), f32),
            pltpu.VMEM((slots, 2, rows, hd), bf16),
            pltpu.VMEM((3, rows, hd), bf16),
            pltpu.VMEM((slots, 3, QUARTERS, SIDE, SIDE, share, quarter), f32),
            pltpu.VMEM((slots, 3, QUARTERS, SIDE, SIDE, share, quarter), f32),
            pltpu.VMEM((slots, 3, QUARTERS, 3, SIDE, share, quarter), f32),
            pltpu.VMEM((slots, 3, QUARTERS, SIDE, share, quarter), f32),
            pltpu.VMEM((slots, 3, QUARTERS, 3, share, quarter), f32),
            pltpu.VMEM((3, 6, 8, 128), f32),
            pltpu.VMEM((2, 3, 6, 8, 128), f32),
            dma((3, slots)),
            dma((spans, PIECES)),
        ]
        + [dma((spans, PIECES)) for _ in range(4)]
        + [dma((slots, PIECES)) for _ in range(2)]
        + [dma((slots, 3, QUARTERS, 3)) for _ in range(8)]
        + [dma((2, 3)), dma((2, 3)), dma((spans, PIECES)), dma((slots, 3))],
        compiler_params=pltpu.CompilerParams(
            collective_id=0, has_side_effects=True, vmem_limit_bytes=67043328
        ),
    )(stream, counts, norm_gain[0], w_qkv[0], w_out[0], fast)
    return (res[None], fin.reshape(1, slots, 1, 3, share, hd))


def solution(mesh):
    in_specs = (
        P(None, "tok", "head"),
        P(),
        P("segment", None, None),
        P("segment", None, None, "head"),
        P("segment", None, "head", None),
        P("segment", None, "head", None, None, None),
    )
    out_specs = (P("segment", None, "tok", "head"), P("segment", None, "head", None, "tok", None))
    return jax.shard_map(body, mesh=mesh, in_specs=in_specs, out_specs=out_specs, check_vma=False)
```

```python
import contextlib
import functools

import jax
import jax.numpy as jnp
from jax import lax
from jax.experimental import pallas as pl
from jax.experimental.pallas import tpu as pltpu
from jax.sharding import PartitionSpec as P

MESH = pl.DeviceIdType.MESH
step_rate = 0.5
tiny = 1e-06
SIDE = 4
QUARTERS = 4
PIECES = 4
PLAN_TWO = (
    "B0", "A3", "B1", "A4", "C0", "B2", "A5", "C1", "D0", "B3", "C2", "D1", "E0", "B4", "C3",
    "D2", "E1", "F0", "B5", "C4", "D3", "E2", "F1", "C5", "D4", "E3", "F2", "D5", "H0", "E4",
    "H1", "F3", "H2",
)
PLAN_TAIL = (
    "E5", "F4", "H3", "F5",
)
PLAN_ONE = (
    "B0", "B1", "C0", "B2", "C1", "D0", "C2", "D1", "E0", "D2", "E1", "F0", "E2", "F1", "H0",
    "F2", "H1", "H2",
)


def mark(name):
    return contextlib.nullcontext()


f32 = jnp.float32
bf16 = jnp.bfloat16


def on(condition, run):
    if condition is True:
        run()
    elif condition is not False:
        pl.when(condition)(run)


def kernel(
    deep,
    stream, counts, gain, wqkv_hbm, wout_hbm, fast_hbm,
    res, fin,
    wqkv, wout, wfast, wb, xin, acc, squares, psend, precv, kv, grads,
    gq, gt, r1, s1, r2, st, st_recv,
    load_sem, x_load, x_send, x_recv, z_send, z_recv, p_send, p_recv,
    rs_send, rs_recv, ag_send, ag_recv,
    st_sem, res_sem, fin_sem,
):
    sections = lax.axis_size("segment")
    s = lax.axis_index("segment")
    t = lax.axis_index("tok")
    h = lax.axis_index("head")
    iy = t // SIDE
    ix = t % SIDE
    piece = xin.shape[4]
    half = piece * PIECES
    width = 2 * half
    hd = wout.shape[1]
    head_scale = hd ** (-0.5)

    def turn(i, d):
        return (i + d + SIDE) % SIDE

    def on_x(d):
        return {"tok": iy * SIDE + turn(ix, d)}

    def on_y(d):
        return {"tok": turn(iy, d) * SIDE + ix}

    partner = {"head": 1 - h}
    above = {"segment": (s + 1) % sections}
    below = {"segment": (s + sections - 1) % sections}

    def load(kind, slot):
        src, dst = ((wqkv_hbm, wqkv), (fast_hbm, wfast), (wout_hbm, wout))[kind]
        return pltpu.make_async_copy(src.at[slot], dst.at[slot], load_sem.at[kind, slot])

    def cols(p, side=0):
        return pl.ds(side * half + p * piece, piece)

    def load_x(span, p):
        return pltpu.make_async_copy(
            stream.at[span, :, cols(p)], xin.at[span, p, h], x_load.at[span, p]
        )

    @pl.when(s == 0)
    def _():
        for span in range(2):
            for p in range(PIECES):
                load_x(span, p).start()

    for slot in range(2):
        for kind in range(3):
            load(kind, slot).start()

    barrier = pltpu.get_barrier_semaphore()
    peers = [partner, above, below]
    for k in range(1, SIDE * SIDE):
        peers.append({"tok": turn(iy, k // SIDE) * SIDE + turn(ix, k % SIDE)})
    for peer in peers:
        pl.semaphore_signal(barrier, inc=1, device_id=peer, device_id_type=MESH)
    pl.semaphore_wait(barrier, len(peers))

    def remote(src, dst, send, recv, device):
        return pltpu.make_async_remote_copy(
            src_ref=src, dst_ref=dst, send_sem=send, recv_sem=recv,
            device_id=device, device_id_type=MESH,
        )

    def hand_up(span, p):
        part = xin.at[span, p, h]
        return remote(part, part, z_send.at[span, p], z_recv.at[span, p], above)

    def share(span, p):
        part = xin.at[span, p, h]
        return remote(part, part, x_send.at[span, p], x_recv.at[span, p], partner)

    def share_in(span, p):
        part = xin.at[span, p, 1 - h]
        return remote(part, part, x_send.at[span, p], x_recv.at[span, p], partner)

    def mix(slot, p):
        return remote(
            psend.at[slot, p], precv.at[slot, p], p_send.at[slot, p], p_recv.at[slot, p], partner
        )

    def result(span, p):
        return pltpu.make_async_copy(
            xin.at[span, p, h], res.at[span, :, cols(p)], res_sem.at[span, p]
        )

    def order(q):
        forward = 1 if q % 2 == 0 else -1
        if q < 2:
            return forward, iy, on_y, ix, on_x
        return forward, ix, on_x, iy, on_y

    def line(buf, slot, m, q, j):
        return buf.at[slot, m, q, j] if q < 2 else buf.at[slot, m, q, :, j]

    def cell(buf, slot, m, q, j):
        if q < 2:
            return buf.at[slot, m, q, iy, j]
        return buf.at[slot, m, q, j, ix]

    def rs1(slot, m, q, k):
        d, i, to, _, _ = order(q)
        j = (turn(i, 2), turn(i, d), turn(i, -d))[k]
        return remote(
            line(gq, slot, m, q, j), r1.at[slot, m, q, k],
            rs_send.at[slot, m, 0], rs_recv.at[slot, m, min(k, 1)], to(d if k < 2 else -d),
        )

    def rs2(slot, m, q, k):
        _, _, _, i, to = order(q)
        return remote(
            s1.at[slot, m, q, turn(i, k + 1)], r2.at[slot, m, q, k],
            rs_send.at[slot, m, 1], rs_recv.at[slot, m, 2], to(k + 1),
        )

    def ag1(slot, m, q, k):
        _, _, _, i, to = order(q)
        part = cell(gt, slot, m, q, i)
        return remote(
            part, part, ag_send.at[slot, m, 0], ag_recv.at[slot, m, 0], to(k + 1)
        )

    def ag2(slot, m, q, k):
        d, i, to, _, _ = order(q)
        part = line(gt, slot, m, q, (i, i, turn(i, -d))[k])
        return remote(
            part, part, ag_send.at[slot, m, 1], ag_recv.at[slot, m, 1 + min(k, 1)], to((d, -d, d)[k])
        )

    def taken(part, sem):
        pltpu.make_async_copy(part, part, sem).wait()

    def rs1_open(slot, m):
        for k in (0, 2):
            for q in range(QUARTERS):
                rs1(slot, m, q, k).start()

    def rs1_pass(slot, m):
        taken(r1.at[slot, m, :, 0], rs_recv.at[slot, m, 0])
        for q in range(QUARTERS):
            d, i, _, _, _ = order(q)
            block = line(gq, slot, m, q, turn(i, d))
            block[...] = block[...] + r1[slot, m, q, 0]
            rs1(slot, m, q, 1).start()

    def rs1_close(slot, m):
        taken(r1.at[slot, m, :, 1:], rs_recv.at[slot, m, 1])
        for q in range(QUARTERS):
            _, i, _, _, _ = order(q)
            s1[slot, m, q] = line(gq, slot, m, q, i)[...] + r1[slot, m, q, 1] + r1[slot, m, q, 2]
            for k in range(3):
                rs2(slot, m, q, k).start()

    def rs2_close(slot, m):
        taken(r2.at[slot, m], rs_recv.at[slot, m, 2])
        for q in range(QUARTERS):
            _, _, _, i, _ = order(q)
            cell(gt, slot, m, q, i)[...] = (
                s1[slot, m, q, i] + r2[slot, m, q, 0] + (r2[slot, m, q, 1] + r2[slot, m, q, 2])
            )

    def ag1_open(slot, m):
        for q in range(QUARTERS):
            for k in range(3):
                ag1(slot, m, q, k).start()

    def ag2_open(slot, m):
        taken(r2.at[slot, m], ag_recv.at[slot, m, 0])
        for q in range(QUARTERS):
            ag2(slot, m, q, 0).start()
            ag2(slot, m, q, 1).start()

    def ag2_pass(slot, m):
        taken(r1.at[slot, m, :, 0], ag_recv.at[slot, m, 1])
        for q in range(QUARTERS):
            ag2(slot, m, q, 2).start()

    def ag2_close(slot, m):
        taken(r1.at[slot, m, :, 1:], ag_recv.at[slot, m, 2])

    def rs_sent(slot, m):
        taken(r1.at[slot, m], rs_send.at[slot, m, 0])
        taken(r2.at[slot, m], rs_send.at[slot, m, 1])

    def ag_sent(slot, m):
        taken(r2.at[slot, m], ag_send.at[slot, m, 0])
        taken(r1.at[slot, m], ag_send.at[slot, m, 1])

    def kept(slot, shape):
        return jnp.broadcast_to(counts[s], shape) > slot

    def update_weights(slot, m):
        def add_squares(b, total):
            part = total
            for q in range(QUARTERS):
                values = gt[slot, m, q, b]
                part = part + jnp.sum(values * values, axis=0)
            return part

        total = lax.fori_loop(0, SIDE, add_squares, jnp.zeros(gt.shape[-2:], f32))
        mean = jnp.sum(total, keepdims=True) / (hd * hd)
        factor = step_rate * lax.rsqrt(mean + tiny)

        def change(b, carry):
            for q in range(QUARTERS):
                lanes = pl.ds(q * 128, 128)
                old = wfast[slot, m, pl.ds(b * SIDE, SIDE), :, lanes]
                new = old - factor * gt[slot, m, q, b]
                new = jnp.where(kept(slot, new.shape), new, old)
                wfast[slot, m, pl.ds(b * SIDE, SIDE), :, lanes] = new
                height = SIDE * new.shape[1]
                wb[slot, m, pl.ds(b * height, height), lanes] = new.reshape(height, -1).astype(bf16)
            return carry

        lax.fori_loop(0, SIDE, change, 0)

    def round_weights(slot):
        for m in range(3):

            def one(b, carry):
                block = wfast[slot, m, pl.ds(b * SIDE, SIDE)]
                height = SIDE * block.shape[1]
                wb[slot, m, pl.ds(b * height, height)] = block.reshape(height, hd).astype(bf16)
                return carry

            lax.fori_loop(0, SIDE, one, 0)

    def finish_weights(slot, m):
        ag2_close(slot, m)
        update_weights(slot, m)
        ag_sent(slot, m)
        rs_sent(slot, m)

    def dot(a, b, dims=((1,), (0,))):
        return lax.dot_general(a, b, (dims, ((), ())), preferred_element_type=f32)

    two = True if all(deep) else sum((s == i).astype(jnp.int32) for i, d in enumerate(deep) if d) > 0
    one = False if two is True else jnp.logical_not(two)

    def qkv_piece(span, slot, p):
        low = xin[span, p, 0]
        high = xin[span, p, 1]
        both = low * low + high * high
        low = (low * gain[slot : slot + 1, cols(p)]).astype(bf16)
        high = (high * gain[slot : slot + 1, cols(p, 1)]).astype(bf16)
        terms = dot(low, wqkv[slot, cols(p)]) + dot(high, wqkv[slot, cols(p, 1)])
        squares[...] = both if p == 0 else squares[...] + both
        acc[...] = terms if p == 0 else acc[...] + terms

    def arrive(span):
        @pl.when(s == 0)
        def _():
            for p in range(PIECES):
                load_x(span, p).wait()
                share(span, p).start()

        for p in range(PIECES):

            @pl.when(s > 0)
            def _():
                with mark("hand"):
                    hand_up(span, p).wait_recv()
                share(span, p).start()

            with mark("share"):
                share_in(span, p).wait_recv()
            if p == 0:

                @pl.when(span == 0)
                def _():
                    load(0, 0).wait()

            with mark("qkv"):
                qkv_piece(span, 0, p)
        for p in range(PIECES):
            share(span, p).wait_send()

    def layer(span, slot):
        mean = jnp.sum(squares[...], axis=-1, keepdims=True) / width
        scale = lax.rsqrt(mean + tiny)
        queries = (acc[:, :hd] * scale).astype(bf16)
        kv[slot, 0] = (acc[:, hd : 2 * hd] * scale).astype(bf16)
        kv[slot, 1] = (acc[:, 2 * hd :] * scale).astype(bf16)

        @pl.when(span == 0)
        def _():
            load(1, slot).wait()
            with mark("round"):
                round_weights(slot)
            load(2, slot).wait()

        if slot == 1:

            @pl.when(span == 1)
            def _():
                with mark("finish1"):
                    finish_weights(1, 1)
                    finish_weights(1, 2)
                for m in range(3):
                    rs1_open(0, m)

        with mark("qmap"):
            gate = dot(queries, wb[slot, 0]) * head_scale
            lift = dot(queries, wb[slot, 1]) * head_scale
            hidden = (gate * jax.nn.sigmoid(gate) * lift).astype(bf16)
            answer = dot(hidden, wb[slot, 2], ((1,), (1,))) * head_scale
            answer_mean = jnp.mean(answer * answer, axis=-1, keepdims=True)
            normed_out = (answer * lax.rsqrt(answer_mean + tiny)).astype(bf16)

        with mark("outp"):
            for p in range(PIECES):
                for side in range(2):
                    psend[slot, p, side] = dot(normed_out, wout[slot, :, cols(p, side)])
                if p % 2 == 1:
                    mix(slot, p - 1).start()
                    mix(slot, p).start()

        with mark("kvpath"):
            keys = kv[slot, 0]
            values = kv[slot, 1]
            gate = dot(keys, wb[slot, 0]) * head_scale
            lift = dot(keys, wb[slot, 1]) * head_scale
            up = dot(values, wb[slot, 2]) * (-head_scale)
            logistic = jax.nn.sigmoid(gate)
            act = gate * logistic
            grads[0] = (up * lift * (logistic * (1.0 + gate * (1.0 - logistic)))).astype(bf16)
            grads[1] = (up * act).astype(bf16)
            grads[2] = (act * lift).astype(bf16)

        with mark("gdots"):
            for m in range(3):
                terms = kv[slot, 0 if m < 2 else 1]
                sign = head_scale if m < 2 else -head_scale
                for e in range(2):
                    part = dot(terms, grads[m, :, e * 256 : (e + 1) * 256], ((0,), (0,))) * sign
                    for f in range(2):
                        gq[slot, m, 2 * e + f] = part[:, f * 128 : (f + 1) * 128].reshape(
                            gq.shape[3:]
                        )
        if slot == 0:

            @pl.when((span == 0) | one)
            def _():
                for m in range(3):
                    rs1_open(slot, m)

        if slot == 0:

            @pl.when(span == 0)
            def _():
                load(0, 1).wait()

        for p in range(PIECES):
            with mark("mixwait"):
                mix(slot, p).wait_recv()
            old = xin[span, p]
            new = old + (psend[slot, p] + precv[slot, p])
            xin[span, p] = jnp.where(kept(slot, new.shape), new, old)

            def leave():
                @pl.when(s < sections - 1)
                def _():
                    hand_up(span, p).start()

                result(span, p).start()

            def go_on():
                with mark("qkv"):
                    qkv_piece(span, 1, p)

            if slot == 0:
                on(two, go_on)
                on(one, leave)
            else:
                leave()
        for p in range(PIECES):
            mix(slot, p).wait_send()

    def run_plan(span, plan):
        def stage(name, unit):
            slot, m = unit // 3, unit % 3
            only_first = {"D": ag1_open, "E": ag2_open, "F": ag2_pass, "H": finish_weights}
            always = {"A": rs1_open, "B": rs1_pass, "C": rs1_close, "D": rs2_close}
            with mark(name + str(unit)):
                if name in always:
                    always[name](slot, m)
                if name in only_first:
                    on(span == 0, lambda: only_first[name](slot, m))

        for step in plan:
            stage(step[0], int(step[1]))

    early = (s == 0) & two

    def phase(k, carry):
        span = jnp.minimum(k, 1)

        @pl.when((k == 0) | ((k == 1) & early) | ((k == 2) & jnp.logical_not(early)))
        def _():
            arrive(span)
            layer(span, 0)

        @pl.when((k != 1) & two)
        def _():
            layer(span, 1)
            run_plan(span, PLAN_TWO)

        @pl.when((k == 1) & two)
        def _():
            run_plan(0, PLAN_TAIL)

        if two is not True:

            @pl.when((k != 1) & one)
            def _():
                run_plan(span, PLAN_ONE)

        return carry

    lax.fori_loop(0, 3, phase, 0)
    for m in range(3):
        rs_sent(0, m)

    def second_sent():
        for m in range(3):
            rs_sent(1, m)

    on(two, second_sent)

    if two is not True:

        @pl.when(one)
        def _():
            load(1, 1).wait()
            load(2, 1).wait()

    def stats(dy, dx):
        k = dy * SIDE + dx
        to = {"tok": turn(iy, dy) * SIDE + turn(ix, dx)}
        return remote(st, st_recv.at[k], st_sem.at[0], st_sem.at[1], to)

    others = [(dy, dx) for dy in range(SIDE) for dx in range(SIDE) if dy or dx]
    st[...] = jnp.zeros(st.shape, f32)

    def own_squares(slot):
        for m in range(3):
            total = jnp.zeros((8, 128), f32)
            for q in range(QUARTERS):
                values = gt[slot, m, q, iy, ix]
                total = total + jnp.sum((values * values).reshape(-1, 8, 128), axis=0)
            u = slot * 3 + m
            st[u : u + 1, :] = jnp.sum(total, axis=0, keepdims=True)

    own_squares(0)
    on(two, lambda: own_squares(1))
    for dy, dx in others:
        stats(dy, dx).start()
    with mark("stats"):
        taken(st_recv.at[1:], st_sem.at[1])
    everyone = st[...]
    for dy, dx in others:
        everyone = everyone + st_recv[dy * SIDE + dx]
    mean = jnp.sum(everyone, axis=-1, keepdims=True) / (hd * hd)
    factors = step_rate * lax.rsqrt(mean + tiny)

    def final(slot, m):
        return pltpu.make_async_copy(wfast.at[slot, m, t], fin.at[slot, m], fin_sem.at[slot, m])

    def last_update(slot):
        for m in range(3):
            factor = factors[slot * 3 + m : slot * 3 + m + 1]
            for q in range(QUARTERS):
                old = wfast[slot, m, t, :, q * 128 : (q + 1) * 128]
                new = old - factor * gt[slot, m, q, iy, ix]
                wfast[slot, m, t, :, q * 128 : (q + 1) * 128] = jnp.where(
                    kept(slot, new.shape), new, old
                )

    last_update(0)
    on(two, lambda: last_update(1))
    for slot in range(2):
        for m in range(3):
            final(slot, m).start()
    for slot in range(2):
        for m in range(3):
            final(slot, m).wait()
    taken(st_recv.at[1:], st_sem.at[0])
    for span in range(2):
        for p in range(PIECES):
            result(span, p).wait()

            @pl.when(s < sections - 1)
            def _():
                hand_up(span, p).wait_send()


def body(stream, counts, norm_gain, w_qkv, w_out, fast_init):
    spans, rows, half = stream.shape
    slots, width, columns = w_qkv.shape[1:]
    hd = fast_init.shape[-1]
    toks = lax.axis_size("tok")
    share = hd // toks
    fast = fast_init.reshape(slots, 3, toks, share, hd)
    piece = half // PIECES
    deep = (True,) * lax.axis_size("segment")
    dma = pltpu.SemaphoreType.DMA
    quarter = hd // QUARTERS
    anywhere = pl.BlockSpec(memory_space=pl.ANY)
    res, fin = pl.pallas_call(
        functools.partial(kernel, deep),
        out_shape=(
            jax.ShapeDtypeStruct((spans, rows, half), f32),
            jax.ShapeDtypeStruct((slots, 3, share, hd), f32),
        ),
        in_specs=[
            anywhere,
            pl.BlockSpec(memory_space=pltpu.SMEM),
            pl.BlockSpec(memory_space=pltpu.VMEM),
            anywhere,
            anywhere,
            anywhere,
        ],
        out_specs=(anywhere, anywhere),
        scratch_shapes=[
            pltpu.VMEM((slots, width, columns), bf16),
            pltpu.VMEM((slots, hd, width), bf16),
            pltpu.VMEM((slots, 3, toks, share, hd), f32),
            pltpu.VMEM((slots, 3, hd, hd), bf16),
            pltpu.VMEM((spans, PIECES, 2, rows, piece), f32),
            pltpu.VMEM((rows, columns), f32),
            pltpu.VMEM((rows, piece), f32),
            pltpu.VMEM((slots, PIECES, 2, rows, piece), f32),
            pltpu.VMEM((slots, PIECES, 2, rows, piece), f32),
            pltpu.VMEM((slots, 2, rows, hd), bf16),
            pltpu.VMEM((3, rows, hd), bf16),
            pltpu.VMEM((slots, 3, QUARTERS, SIDE, SIDE, share, quarter), f32),
            pltpu.VMEM((slots, 3, QUARTERS, SIDE, SIDE, share, quarter), f32),
            pltpu.VMEM((slots, 3, QUARTERS, 3, SIDE, share, quarter), f32),
            pltpu.VMEM((slots, 3, QUARTERS, SIDE, share, quarter), f32),
            pltpu.VMEM((slots, 3, QUARTERS, 3, share, quarter), f32),
            pltpu.VMEM((8, 128), f32),
            pltpu.VMEM((SIDE * SIDE, 8, 128), f32),
            dma((3, slots)),
            dma((spans, PIECES)),
        ]
        + [dma((spans, PIECES)) for _ in range(4)]
        + [dma((slots, PIECES)) for _ in range(2)]
        + [dma((slots, 3, n)) for n in (2, 3, 2, 3)]
        + [dma((2,)), dma((spans, PIECES)), dma((slots, 3))],
        compiler_params=pltpu.CompilerParams(
            collective_id=0, has_side_effects=True, vmem_limit_bytes=67043328
        ),
    )(stream, counts, norm_gain[0], w_qkv[0], w_out[0], fast)
    return (res[None], fin.reshape(1, slots, 1, 3, share, hd))


def solution(mesh):
    in_specs = (
        P(None, "tok", "head"),
        P(),
        P("segment", None, None),
        P("segment", None, None, "head"),
        P("segment", None, "head", None),
        P("segment", None, "head", None, None, None),
    )
    out_specs = (P("segment", None, "tok", "head"), P("segment", None, "head", None, "tok", None))
    return jax.shard_map(body, mesh=mesh, in_specs=in_specs, out_specs=out_specs, check_vma=False)
```

```python
import contextlib
import functools

import jax
import jax.numpy as jnp
from jax import lax
from jax.experimental import pallas as pl
from jax.experimental.pallas import tpu as pltpu
from jax.sharding import PartitionSpec as P

MESH = pl.DeviceIdType.MESH
step_rate = 0.5
tiny = 1e-06
SIDE = 4
QUARTERS = 4
PIECES = 4
PLAN_TWO = (
    "B0", "A3", "B1", "A4", "B2", "C0", "A5", "C1", "D0", "B3", "C2", "D1", "E0", "B4", "C3",
    "D2", "E1", "F0", "B5", "C4", "D3", "E2", "F1", "C5", "D4", "E3", "F2", "D5", "H0", "E4",
    "H1", "F3", "E5",
)
PLAN_MIDDLE = (
    "H2", "F4",
)
PLAN_TAIL = (
    "H3", "F5",
)
PLAN_ONE = (
    "B0", "B1", "C0", "B2", "C1", "D0", "C2", "D1", "E0", "D2", "E1", "F0", "E2", "F1", "H0",
    "F2", "H1", "H2",
)


def mark(name):
    return contextlib.nullcontext()


f32 = jnp.float32
bf16 = jnp.bfloat16


def on(condition, run):
    if condition is True:
        run()
    elif condition is not False:
        pl.when(condition)(run)


def kernel(
    deep,
    stream, counts, gain, wqkv_hbm, wout_hbm, fast_hbm,
    res, fin,
    wqkv, wout, wfast, wb, xin, acc, squares, psend, precv, kv, grads,
    gq, gt, r1, s1, r2, st, st_recv,
    load_sem, x_load, x_send, x_recv, z_send, z_recv, p_send, p_recv,
    rs_send, rs_recv, ag_send, ag_recv,
    st_sem, res_sem, fin_sem,
):
    sections = lax.axis_size("segment")
    s = lax.axis_index("segment")
    t = lax.axis_index("tok")
    h = lax.axis_index("head")
    iy = t // SIDE
    ix = t % SIDE
    piece = xin.shape[4]
    half = piece * PIECES
    width = 2 * half
    hd = wout.shape[1]
    head_scale = hd ** (-0.5)

    def turn(i, d):
        return (i + d + SIDE) % SIDE

    def on_x(d):
        return {"tok": iy * SIDE + turn(ix, d)}

    def on_y(d):
        return {"tok": turn(iy, d) * SIDE + ix}

    partner = {"head": 1 - h}
    above = {"segment": (s + 1) % sections}
    below = {"segment": (s + sections - 1) % sections}

    def load(kind, slot):
        src, dst = ((wqkv_hbm, wqkv), (fast_hbm, wfast), (wout_hbm, wout))[kind]
        return pltpu.make_async_copy(src.at[slot], dst.at[slot], load_sem.at[kind, slot])

    def cols(p, side=0):
        return pl.ds(side * half + p * piece, piece)

    def load_x(span, p):
        return pltpu.make_async_copy(
            stream.at[span, :, cols(p)], xin.at[span, p, h], x_load.at[span, p]
        )

    @pl.when(s == 0)
    def _():
        for span in range(2):
            for p in range(PIECES):
                load_x(span, p).start()

    for slot in range(2):
        for kind in range(3):
            load(kind, slot).start()

    barrier = pltpu.get_barrier_semaphore()
    peers = [partner, above, below]
    for d in (1, 3):
        peers += [on_x(d), on_y(d)]
    for peer in peers:
        pl.semaphore_signal(barrier, inc=1, device_id=peer, device_id_type=MESH)
    pl.semaphore_wait(barrier, len(peers))

    def remote(src, dst, send, recv, device):
        return pltpu.make_async_remote_copy(
            src_ref=src, dst_ref=dst, send_sem=send, recv_sem=recv,
            device_id=device, device_id_type=MESH,
        )

    def hand_up(span, p):
        part = xin.at[span, p, h]
        return remote(part, part, z_send.at[span, p], z_recv.at[span, p], above)

    def share(span, p):
        part = xin.at[span, p, h]
        return remote(part, part, x_send.at[span, p], x_recv.at[span, p], partner)

    def share_in(span, p):
        part = xin.at[span, p, 1 - h]
        return remote(part, part, x_send.at[span, p], x_recv.at[span, p], partner)

    def mix(slot, p):
        return remote(
            psend.at[slot, p], precv.at[slot, p], p_send.at[slot, p], p_recv.at[slot, p], partner
        )

    def result(span, p):
        return pltpu.make_async_copy(
            xin.at[span, p, h], res.at[span, :, cols(p)], res_sem.at[span, p]
        )

    def order(q):
        forward = 1 if q % 2 == 0 else -1
        if q < 2:
            return forward, iy, on_y, ix, on_x
        return forward, ix, on_x, iy, on_y

    def line(buf, slot, m, q, j):
        return buf.at[slot, m, q, j] if q < 2 else buf.at[slot, m, q, :, j]

    def cell(buf, slot, m, q, j):
        if q < 2:
            return buf.at[slot, m, q, iy, j]
        return buf.at[slot, m, q, j, ix]

    def rs1(slot, m, q, k):
        d, i, to, _, _ = order(q)
        j = (turn(i, 2), turn(i, d), turn(i, -d))[k]
        return remote(
            line(gq, slot, m, q, j), r1.at[slot, m, q, k],
            rs_send.at[slot, m, 0], rs_recv.at[slot, m, min(k, 1)], to(d if k < 2 else -d),
        )

    def rs2(slot, m, q, k):
        _, _, _, i, to = order(q)
        return remote(
            s1.at[slot, m, q, turn(i, k + 1)], r2.at[slot, m, q, k],
            rs_send.at[slot, m, 1], rs_recv.at[slot, m, 2], to(k + 1),
        )

    def ag1(slot, m, q, k):
        _, _, _, i, to = order(q)
        part = cell(gt, slot, m, q, i)
        return remote(
            part, part, ag_send.at[slot, m, 0], ag_recv.at[slot, m, 0], to(k + 1)
        )

    def ag2(slot, m, q, k):
        d, i, to, _, _ = order(q)
        part = line(gt, slot, m, q, (i, i, turn(i, -d))[k])
        return remote(
            part, part, ag_send.at[slot, m, 1], ag_recv.at[slot, m, 1 + min(k, 1)], to((d, -d, d)[k])
        )

    def taken(part, sem):
        pltpu.make_async_copy(part, part, sem).wait()

    def rs1_open(slot, m):
        for k in (0, 2):
            for q in range(QUARTERS):
                rs1(slot, m, q, k).start()

    def rs1_pass(slot, m):
        taken(r1.at[slot, m, :, 0], rs_recv.at[slot, m, 0])
        for q in range(QUARTERS):
            d, i, _, _, _ = order(q)
            block = line(gq, slot, m, q, turn(i, d))
            block[...] = block[...] + r1[slot, m, q, 0]
            rs1(slot, m, q, 1).start()

    def rs1_close(slot, m):
        taken(r1.at[slot, m, :, 1:], rs_recv.at[slot, m, 1])
        for q in range(QUARTERS):
            _, i, _, _, _ = order(q)
            s1[slot, m, q] = line(gq, slot, m, q, i)[...] + r1[slot, m, q, 1] + r1[slot, m, q, 2]
            for k in range(3):
                rs2(slot, m, q, k).start()

    def rs2_close(slot, m):
        taken(r2.at[slot, m], rs_recv.at[slot, m, 2])
        for q in range(QUARTERS):
            _, _, _, i, _ = order(q)
            cell(gt, slot, m, q, i)[...] = (
                s1[slot, m, q, i] + r2[slot, m, q, 0] + (r2[slot, m, q, 1] + r2[slot, m, q, 2])
            )

    def ag1_open(slot, m):
        for q in range(QUARTERS):
            for k in range(3):
                ag1(slot, m, q, k).start()

    def ag2_open(slot, m):
        taken(r2.at[slot, m], ag_recv.at[slot, m, 0])
        for q in range(QUARTERS):
            ag2(slot, m, q, 0).start()
            ag2(slot, m, q, 1).start()

    def ag2_pass(slot, m):
        taken(r1.at[slot, m, :, 0], ag_recv.at[slot, m, 1])
        for q in range(QUARTERS):
            ag2(slot, m, q, 2).start()

    def ag2_close(slot, m):
        taken(r1.at[slot, m, :, 1:], ag_recv.at[slot, m, 2])

    def rs_sent(slot, m):
        taken(r1.at[slot, m], rs_send.at[slot, m, 0])
        taken(r2.at[slot, m], rs_send.at[slot, m, 1])

    def ag_sent(slot, m):
        taken(r2.at[slot, m], ag_send.at[slot, m, 0])
        taken(r1.at[slot, m], ag_send.at[slot, m, 1])

    def kept(slot, shape):
        return jnp.broadcast_to(counts[s], shape) > slot

    def update_weights(slot, m):
        def add_squares(b, total):
            part = total
            for q in range(QUARTERS):
                values = gt[slot, m, q, b]
                part = part + jnp.sum(values * values, axis=0)
            return part

        total = lax.fori_loop(0, SIDE, add_squares, jnp.zeros(gt.shape[-2:], f32))
        mean = jnp.sum(total, keepdims=True) / (hd * hd)
        factor = step_rate * lax.rsqrt(mean + tiny)

        def change(b, carry):
            for q in range(QUARTERS):
                lanes = pl.ds(q * 128, 128)
                old = wfast[slot, m, pl.ds(b * SIDE, SIDE), :, lanes]
                new = old - factor * gt[slot, m, q, b]
                new = jnp.where(kept(slot, new.shape), new, old)
                wfast[slot, m, pl.ds(b * SIDE, SIDE), :, lanes] = new
                height = SIDE * new.shape[1]
                wb[slot, m, pl.ds(b * height, height), lanes] = new.reshape(height, -1).astype(bf16)
            return carry

        lax.fori_loop(0, SIDE, change, 0)

    def round_weights(slot):
        for m in range(3):

            def one(b, carry):
                block = wfast[slot, m, pl.ds(b * SIDE, SIDE)]
                height = SIDE * block.shape[1]
                wb[slot, m, pl.ds(b * height, height)] = block.reshape(height, hd).astype(bf16)
                return carry

            lax.fori_loop(0, SIDE, one, 0)

    def finish_weights(slot, m):
        ag2_close(slot, m)
        update_weights(slot, m)
        ag_sent(slot, m)
        rs_sent(slot, m)

    def dot(a, b, dims=((1,), (0,))):
        return lax.dot_general(a, b, (dims, ((), ())), preferred_element_type=f32)

    two = True if all(deep) else sum((s == i).astype(jnp.int32) for i, d in enumerate(deep) if d) > 0
    one = False if two is True else jnp.logical_not(two)
    early = (s == 0) & two

    def qkv_piece(span, slot, p):
        low = xin[span, p, 0]
        high = xin[span, p, 1]
        both = low * low + high * high
        low = (low * gain[slot : slot + 1, cols(p)]).astype(bf16)
        high = (high * gain[slot : slot + 1, cols(p, 1)]).astype(bf16)
        terms = dot(low, wqkv[slot, cols(p)]) + dot(high, wqkv[slot, cols(p, 1)])
        squares[...] = both if p == 0 else squares[...] + both
        acc[...] = terms if p == 0 else acc[...] + terms

    def arrive(span):
        @pl.when(s == 0)
        def _():
            for p in range(PIECES):
                load_x(span, p).wait()
                share(span, p).start()

        for p in range(PIECES):

            @pl.when(s > 0)
            def _():
                with mark("hand"):
                    hand_up(span, p).wait_recv()
                share(span, p).start()

            with mark("share"):
                share_in(span, p).wait_recv()
            if p == 0:

                @pl.when(span == 0)
                def _():
                    load(0, 0).wait()

            with mark("qkv"):
                qkv_piece(span, 0, p)
        for p in range(PIECES):
            share(span, p).wait_send()

    def layer(span, slot):
        mean = jnp.sum(squares[...], axis=-1, keepdims=True) / width
        scale = lax.rsqrt(mean + tiny)
        queries = (acc[:, :hd] * scale).astype(bf16)
        kv[slot, 0] = (acc[:, hd : 2 * hd] * scale).astype(bf16)
        kv[slot, 1] = (acc[:, 2 * hd :] * scale).astype(bf16)

        @pl.when(span == 0)
        def _():
            load(1, slot).wait()
            with mark("round"):
                round_weights(slot)
            load(2, slot).wait()

        if slot == 1:

            @pl.when(span == 1)
            def _():
                with mark("finish1"):
                    finish_weights(1, 1)
                    finish_weights(1, 2)

            @pl.when((span == 1) & early)
            def _():
                for m in range(3):
                    rs1_open(0, m)

        with mark("qmap"):
            gate = dot(queries, wb[slot, 0]) * head_scale
            lift = dot(queries, wb[slot, 1]) * head_scale
            hidden = (gate * jax.nn.sigmoid(gate) * lift).astype(bf16)
            answer = dot(hidden, wb[slot, 2], ((1,), (1,))) * head_scale
            answer_mean = jnp.mean(answer * answer, axis=-1, keepdims=True)
            normed_out = (answer * lax.rsqrt(answer_mean + tiny)).astype(bf16)

        with mark("outp"):
            for p in range(PIECES):
                for side in range(2):
                    psend[slot, p, side] = dot(normed_out, wout[slot, :, cols(p, side)])
                if p % 2 == 1:
                    mix(slot, p - 1).start()
                    mix(slot, p).start()

        with mark("kvpath"):
            keys = kv[slot, 0]
            values = kv[slot, 1]
            gate = dot(keys, wb[slot, 0]) * head_scale
            lift = dot(keys, wb[slot, 1]) * head_scale
            up = dot(values, wb[slot, 2]) * (-head_scale)
            logistic = jax.nn.sigmoid(gate)
            act = gate * logistic
            grads[0] = (up * lift * (logistic * (1.0 + gate * (1.0 - logistic)))).astype(bf16)
            grads[1] = (up * act).astype(bf16)
            grads[2] = (act * lift).astype(bf16)

        with mark("gdots"):
            for m in range(3):
                terms = kv[slot, 0 if m < 2 else 1]
                sign = head_scale if m < 2 else -head_scale
                for e in range(2):
                    part = dot(terms, grads[m, :, e * 256 : (e + 1) * 256], ((0,), (0,))) * sign
                    for f in range(2):
                        gq[slot, m, 2 * e + f] = part[:, f * 128 : (f + 1) * 128].reshape(
                            gq.shape[3:]
                        )
        if slot == 0:

            @pl.when((span == 0) | jnp.logical_not(early))
            def _():
                for m in range(3):
                    rs1_open(slot, m)

        if slot == 0:

            @pl.when(span == 0)
            def _():
                load(0, 1).wait()

        for p in range(PIECES):
            with mark("mixwait"):
                mix(slot, p).wait_recv()
            old = xin[span, p]
            new = old + (psend[slot, p] + precv[slot, p])
            xin[span, p] = jnp.where(kept(slot, new.shape), new, old)

            def leave():
                @pl.when(s < sections - 1)
                def _():
                    hand_up(span, p).start()

                result(span, p).start()

            def go_on():
                with mark("qkv"):
                    qkv_piece(span, 1, p)

            if slot == 0:
                on(two, go_on)
                on(one, leave)
            else:
                leave()
        for p in range(PIECES):
            mix(slot, p).wait_send()

    def run_plan(span, plan):
        def stage(name, unit):
            slot, m = unit // 3, unit % 3
            only_first = {"D": ag1_open, "E": ag2_open, "F": ag2_pass, "H": finish_weights}
            always = {"A": rs1_open, "B": rs1_pass, "C": rs1_close, "D": rs2_close}
            with mark(name + str(unit)):
                if name in always:
                    always[name](slot, m)
                if name in only_first:
                    on(span == 0, lambda: only_first[name](slot, m))

        for step in plan:
            stage(step[0], int(step[1]))

    def phase(k, carry):
        span = jnp.minimum(k, 1)

        now = (k == 0) | ((k == 1) & early) | ((k == 2) & jnp.logical_not(early))

        @pl.when(now)
        def _():
            arrive(span)

        @pl.when((k == 1) & two)
        def _():
            run_plan(0, PLAN_MIDDLE)

        @pl.when(now)
        def _():
            layer(span, 0)

        @pl.when((k != 1) & two)
        def _():
            layer(span, 1)
            run_plan(span, PLAN_TWO)

        @pl.when((k == 1) & two)
        def _():
            run_plan(0, PLAN_TAIL)

        if two is not True:

            @pl.when((k != 1) & one)
            def _():
                run_plan(span, PLAN_ONE)

        return carry

    lax.fori_loop(0, 3, phase, 0)
    for m in range(3):
        rs_sent(0, m)

    def second_sent():
        for m in range(3):
            rs_sent(1, m)

    on(two, second_sent)

    if two is not True:

        @pl.when(one)
        def _():
            load(1, 1).wait()
            load(2, 1).wait()

    def stats(dy, dx):
        k = dy * SIDE + dx
        to = {"tok": turn(iy, dy) * SIDE + turn(ix, dx)}
        return remote(st, st_recv.at[k], st_sem.at[0], st_sem.at[1], to)

    others = [(dy, dx) for dy in range(SIDE) for dx in range(SIDE) if dy or dx]
    st[...] = jnp.zeros(st.shape, f32)

    def own_squares(slot):
        for m in range(3):
            total = jnp.zeros((8, 128), f32)
            for q in range(QUARTERS):
                values = gt[slot, m, q, iy, ix]
                total = total + jnp.sum((values * values).reshape(-1, 8, 128), axis=0)
            u = slot * 3 + m
            st[u : u + 1, :] = jnp.sum(total, axis=0, keepdims=True)

    own_squares(0)
    on(two, lambda: own_squares(1))
    for dy, dx in others:
        stats(dy, dx).start()
    with mark("stats"):
        taken(st_recv.at[1:], st_sem.at[1])
    everyone = st[...]
    for dy, dx in others:
        everyone = everyone + st_recv[dy * SIDE + dx]
    mean = jnp.sum(everyone, axis=-1, keepdims=True) / (hd * hd)
    factors = step_rate * lax.rsqrt(mean + tiny)

    def final(slot, m):
        return pltpu.make_async_copy(wfast.at[slot, m, t], fin.at[slot, m], fin_sem.at[slot, m])

    def last_update(slot):
        for m in range(3):
            factor = factors[slot * 3 + m : slot * 3 + m + 1]
            for q in range(QUARTERS):
                old = wfast[slot, m, t, :, q * 128 : (q + 1) * 128]
                new = old - factor * gt[slot, m, q, iy, ix]
                wfast[slot, m, t, :, q * 128 : (q + 1) * 128] = jnp.where(
                    kept(slot, new.shape), new, old
                )

    last_update(0)
    on(two, lambda: last_update(1))
    for slot in range(2):
        for m in range(3):
            final(slot, m).start()
    for slot in range(2):
        for m in range(3):
            final(slot, m).wait()
    taken(st_recv.at[1:], st_sem.at[0])
    for span in range(2):
        for p in range(PIECES):
            result(span, p).wait()

            @pl.when(s < sections - 1)
            def _():
                hand_up(span, p).wait_send()


def body(stream, counts, norm_gain, w_qkv, w_out, fast_init):
    spans, rows, half = stream.shape
    slots, width, columns = w_qkv.shape[1:]
    hd = fast_init.shape[-1]
    toks = lax.axis_size("tok")
    share = hd // toks
    fast = fast_init.reshape(slots, 3, toks, share, hd)
    piece = half // PIECES
    deep = (True,) * lax.axis_size("segment")
    dma = pltpu.SemaphoreType.DMA
    quarter = hd // QUARTERS
    anywhere = pl.BlockSpec(memory_space=pl.ANY)
    res, fin = pl.pallas_call(
        functools.partial(kernel, deep),
        out_shape=(
            jax.ShapeDtypeStruct((spans, rows, half), f32),
            jax.ShapeDtypeStruct((slots, 3, share, hd), f32),
        ),
        in_specs=[
            anywhere,
            pl.BlockSpec(memory_space=pltpu.SMEM),
            pl.BlockSpec(memory_space=pltpu.VMEM),
            anywhere,
            anywhere,
            anywhere,
        ],
        out_specs=(anywhere, anywhere),
        scratch_shapes=[
            pltpu.VMEM((slots, width, columns), bf16),
            pltpu.VMEM((slots, hd, width), bf16),
            pltpu.VMEM((slots, 3, toks, share, hd), f32),
            pltpu.VMEM((slots, 3, hd, hd), bf16),
            pltpu.VMEM((spans, PIECES, 2, rows, piece), f32),
            pltpu.VMEM((rows, columns), f32),
            pltpu.VMEM((rows, piece), f32),
            pltpu.VMEM((slots, PIECES, 2, rows, piece), f32),
            pltpu.VMEM((slots, PIECES, 2, rows, piece), f32),
            pltpu.VMEM((slots, 2, rows, hd), bf16),
            pltpu.VMEM((3, rows, hd), bf16),
            pltpu.VMEM((slots, 3, QUARTERS, SIDE, SIDE, share, quarter), f32),
            pltpu.VMEM((slots, 3, QUARTERS, SIDE, SIDE, share, quarter), f32),
            pltpu.VMEM((slots, 3, QUARTERS, 3, SIDE, share, quarter), f32),
            pltpu.VMEM((slots, 3, QUARTERS, SIDE, share, quarter), f32),
            pltpu.VMEM((slots, 3, QUARTERS, 3, share, quarter), f32),
            pltpu.VMEM((8, 128), f32),
            pltpu.VMEM((SIDE * SIDE, 8, 128), f32),
            dma((3, slots)),
            dma((spans, PIECES)),
        ]
        + [dma((spans, PIECES)) for _ in range(4)]
        + [dma((slots, PIECES)) for _ in range(2)]
        + [dma((slots, 3, n)) for n in (2, 3, 2, 3)]
        + [dma((2,)), dma((spans, PIECES)), dma((slots, 3))],
        compiler_params=pltpu.CompilerParams(
            collective_id=0, has_side_effects=True, vmem_limit_bytes=67043328
        ),
    )(stream, counts, norm_gain[0], w_qkv[0], w_out[0], fast)
    return (res[None], fin.reshape(1, slots, 1, 3, share, hd))


def solution(mesh):
    in_specs = (
        P(None, "tok", "head"),
        P(),
        P("segment", None, None),
        P("segment", None, None, "head"),
        P("segment", None, "head", None),
        P("segment", None, "head", None, None, None),
    )
    out_specs = (P("segment", None, "tok", "head"), P("segment", None, "head", None, "tok", None))
    return jax.shard_map(body, mesh=mesh, in_specs=in_specs, out_specs=out_specs, check_vma=False)
```

```python
import contextlib
import functools

import jax
import jax.numpy as jnp
from jax import lax
from jax.experimental import pallas as pl
from jax.experimental.pallas import tpu as pltpu
from jax.sharding import PartitionSpec as P

MESH = pl.DeviceIdType.MESH
step_rate = 0.5
tiny = 1e-06
SIDE = 4
QUARTERS = 4
FREE = 2
PIECES = 4
PLAN_TWO = (
    "B0", "A3", "B1", "A4", "B2", "A5", "C0", "B3", "C1", "B4", "C2", "B5", "D0", "C3", "D1",
    "E0", "C4", "D2", "E1", "F0", "C5", "D3", "E2", "F1", "D4", "E3", "F2", "D5", "H0", "E4",
    "H1",
)
PLAN_MIDDLE = (
    "F3", "E5", "H2", "F4",
)
PLAN_TAIL = (
    "F5", "H3",
)
PLAN_ONE = (
    "B0", "B1", "B2", "C0", "C1", "C2", "D0", "E0", "D1", "E1", "D2", "E2", "F0", "F1", "F2",
    "H0", "H1", "H2",
)


def mark(name):
    return contextlib.nullcontext()


f32 = jnp.float32
bf16 = jnp.bfloat16


def on(condition, run):
    if condition is True:
        run()
    elif condition is not False:
        pl.when(condition)(run)


def kernel(
    deep,
    stream, counts, gain, wqkv_hbm, wout_hbm, fast_hbm,
    res, fin,
    wqkv, wout, wfast, wb, xin, acc, squares, psend, precv, kv, grads,
    gq, gt, r1, s1, r2, st, st_recv,
    load_sem, x_load, x_send, x_recv, z_send, z_recv, p_send, p_recv,
    rs_send, rs_recv, ag_send, ag_recv,
    st_sem, res_sem, fin_sem,
):
    sections = lax.axis_size("segment")
    s = lax.axis_index("segment")
    t = lax.axis_index("tok")
    h = lax.axis_index("head")
    iy = t // SIDE
    ix = t % SIDE
    piece = xin.shape[4]
    half = piece * PIECES
    width = 2 * half
    hd = wout.shape[1]
    head_scale = hd ** (-0.5)

    def turn(i, d):
        return (i + d + SIDE) % SIDE

    def on_x(d):
        return {"tok": iy * SIDE + turn(ix, d)}

    def on_y(d):
        return {"tok": turn(iy, d) * SIDE + ix}

    partner = {"head": 1 - h}
    above = {"segment": (s + 1) % sections}
    below = {"segment": (s + sections - 1) % sections}

    def load(kind, slot):
        src, dst = ((wqkv_hbm, wqkv), (fast_hbm, wfast), (wout_hbm, wout))[kind]
        return pltpu.make_async_copy(src.at[slot], dst.at[slot], load_sem.at[kind, slot])

    def cols(p, side=0):
        return pl.ds(side * half + p * piece, piece)

    def load_x(span, p):
        return pltpu.make_async_copy(
            stream.at[span, :, cols(p)], xin.at[span, p, h], x_load.at[span, p]
        )

    @pl.when(s == 0)
    def _():
        for span in range(2):
            for p in range(PIECES):
                load_x(span, p).start()

    for slot in range(2):
        for kind in range(3):
            load(kind, slot).start()

    barrier = pltpu.get_barrier_semaphore()
    peers = [partner, above, below]
    for d in (1, 3):
        peers += [on_x(d), on_y(d)]
    for peer in peers:
        pl.semaphore_signal(barrier, inc=1, device_id=peer, device_id_type=MESH)
    pl.semaphore_wait(barrier, len(peers))

    def remote(src, dst, send, recv, device):
        return pltpu.make_async_remote_copy(
            src_ref=src, dst_ref=dst, send_sem=send, recv_sem=recv,
            device_id=device, device_id_type=MESH,
        )

    def hand_up(span, p):
        part = xin.at[span, p, h]
        return remote(part, part, z_send.at[span, p], z_recv.at[span, p], above)

    def share(span, p):
        part = xin.at[span, p, h]
        return remote(part, part, x_send.at[span, p], x_recv.at[span, p], partner)

    def share_in(span, p):
        part = xin.at[span, p, 1 - h]
        return remote(part, part, x_send.at[span, p], x_recv.at[span, p], partner)

    def mix(slot, p):
        return remote(
            psend.at[slot, p], precv.at[slot, p], p_send.at[slot, p], p_recv.at[slot, p], partner
        )

    def result(span, p):
        return pltpu.make_async_copy(
            xin.at[span, p, h], res.at[span, :, cols(p)], res_sem.at[span, p]
        )

    def order(q):
        forward = 1 if q % 2 == 0 else -1
        if q < 2:
            return forward, iy, on_y, ix, on_x
        return forward, ix, on_x, iy, on_y

    def line(buf, slot, m, q, j):
        return buf.at[slot, m, q, j] if q < 2 else buf.at[slot, m, q, :, j]

    def cell(buf, slot, m, q, j):
        if q < 2:
            return buf.at[slot, m, q, iy, j]
        return buf.at[slot, m, q, j, ix]

    def rs1(slot, m, q, k):
        d, i, to, _, _ = order(q)
        j = (turn(i, 2), turn(i, d), turn(i, -d))[k]
        return remote(
            line(gq, slot, m, q, j), r1.at[slot, m, q, k],
            rs_send.at[slot, m, 0], rs_recv.at[slot, m, min(k, 1)], to(d if k < 2 else -d),
        )

    def rs2(slot, m, q, k):
        _, _, _, i, to = order(q)
        return remote(
            s1.at[slot, m, q, turn(i, k + 1)], r2.at[slot, m, q, k],
            rs_send.at[slot, m, 1], rs_recv.at[slot, m, 2], to(k + 1),
        )

    def ag1(slot, m, q, k):
        _, _, _, i, to = order(q)
        part = cell(gt, slot, m, q, i)
        return remote(
            part, part, ag_send.at[slot, m, 0], ag_recv.at[slot, m, 0], to(k + 1)
        )

    def ag2(slot, m, q, k):
        d, i, to, _, _ = order(q)
        part = line(gt, slot, m, q, (i, i, turn(i, -d))[k])
        return remote(
            part, part, ag_send.at[slot, m, 1], ag_recv.at[slot, m, 1 + min(k, 1)], to((d, -d, d)[k])
        )

    def taken(part, sem):
        pltpu.make_async_copy(part, part, sem).wait()

    def rs1_open(slot, m):
        for k in (0, 2):
            for q in range(QUARTERS):
                rs1(slot, m, q, k).start()

    def rs1_pass(slot, m):
        taken(r1.at[slot, m, :, 0], rs_recv.at[slot, m, 0])
        for q in range(QUARTERS):
            d, i, _, _, _ = order(q)
            block = line(gq, slot, m, q, turn(i, d))
            block[...] = block[...] + r1[slot, m, q, 0]
            rs1(slot, m, q, 1).start()

    def rs1_close(slot, m):
        taken(r1.at[slot, m, :, 1:], rs_recv.at[slot, m, 1])
        for q in range(QUARTERS):
            _, i, _, _, _ = order(q)
            s1[slot, m, q] = line(gq, slot, m, q, i)[...] + r1[slot, m, q, 1] + r1[slot, m, q, 2]
            for k in range(3):
                rs2(slot, m, q, k).start()

    def rs2_close(slot, m):
        taken(r2.at[slot, m], rs_recv.at[slot, m, 2])
        for q in range(QUARTERS):
            _, _, _, i, _ = order(q)
            cell(gt, slot, m, q, i)[...] = (
                s1[slot, m, q, i] + r2[slot, m, q, 0] + (r2[slot, m, q, 1] + r2[slot, m, q, 2])
            )

    def ag1_open(slot, m):
        for q in range(QUARTERS):
            for k in range(3):
                ag1(slot, m, q, k).start()

    def ag2_open(slot, m):
        taken(r2.at[slot, m], ag_recv.at[slot, m, 0])
        for q in range(QUARTERS):
            ag2(slot, m, q, 0).start()
            ag2(slot, m, q, 1).start()

    def ag2_pass(slot, m):
        taken(r1.at[slot, m, :, 0], ag_recv.at[slot, m, 1])
        for q in range(QUARTERS):
            ag2(slot, m, q, 2).start()

    def ag2_close(slot, m):
        taken(r1.at[slot, m, :, 1:], ag_recv.at[slot, m, 2])

    def rs_sent(slot, m):
        taken(r1.at[slot, m], rs_send.at[slot, m, 0])
        taken(r2.at[slot, m], rs_send.at[slot, m, 1])

    def ag_sent(slot, m):
        taken(r2.at[slot, m], ag_send.at[slot, m, 0])
        taken(r1.at[slot, m], ag_send.at[slot, m, 1])

    def kept(slot, shape):
        return jnp.broadcast_to(counts[s], shape) > slot

    def update_weights(slot, m):
        def add_squares(b, total):
            part = total
            for q in range(QUARTERS):
                values = gt[slot, m, q, b]
                part = part + jnp.sum(values * values, axis=0)
            return part

        total = lax.fori_loop(0, SIDE, add_squares, jnp.zeros(gt.shape[-2:], f32))
        mean = jnp.sum(total, keepdims=True) / (hd * hd)
        factor = step_rate * lax.rsqrt(mean + tiny)

        def change(b, carry):
            for q in range(QUARTERS):
                lanes = pl.ds(q * 128, 128)
                old = wfast[slot, m, pl.ds(b * SIDE, SIDE), :, lanes]
                new = old - factor * gt[slot, m, q, b]
                new = jnp.where(kept(slot, new.shape), new, old)
                wfast[slot, m, pl.ds(b * SIDE, SIDE), :, lanes] = new
                height = SIDE * new.shape[1]
                wb[slot, m, pl.ds(b * height, height), lanes] = new.reshape(height, -1).astype(bf16)
            return carry

        lax.fori_loop(0, SIDE, change, 0)

    def round_weights(slot):
        for m in range(3):

            def one(b, carry):
                block = wfast[slot, m, pl.ds(b * SIDE, SIDE)]
                height = SIDE * block.shape[1]
                wb[slot, m, pl.ds(b * height, height)] = block.reshape(height, hd).astype(bf16)
                return carry

            lax.fori_loop(0, SIDE, one, 0)

    def finish_weights(slot, m):
        ag2_close(slot, m)
        update_weights(slot, m)
        ag_sent(slot, m)
        rs_sent(slot, m)

    def dot(a, b, dims=((1,), (0,))):
        return lax.dot_general(a, b, (dims, ((), ())), preferred_element_type=f32)

    two = True if all(deep) else sum((s == i).astype(jnp.int32) for i, d in enumerate(deep) if d) > 0
    one = False if two is True else jnp.logical_not(two)
    early = (s == 0) & two

    def qkv_piece(span, slot, p):
        low = xin[span, p, 0]
        high = xin[span, p, 1]
        both = low * low + high * high
        low = (low * gain[slot : slot + 1, cols(p)]).astype(bf16)
        high = (high * gain[slot : slot + 1, cols(p, 1)]).astype(bf16)
        terms = dot(low, wqkv[slot, cols(p)]) + dot(high, wqkv[slot, cols(p, 1)])
        squares[...] = both if p == 0 else squares[...] + both
        acc[...] = terms if p == 0 else acc[...] + terms

    def arrive(span):
        @pl.when(s == 0)
        def _():
            for p in range(PIECES):
                load_x(span, p).wait()
                share(span, p).start()

        for p in range(PIECES):

            @pl.when(s > 0)
            def _():
                with mark("hand"):
                    hand_up(span, p).wait_recv()
                share(span, p).start()

            with mark("share"):
                share_in(span, p).wait_recv()
            if p == 0:

                @pl.when(span == 0)
                def _():
                    load(0, 0).wait()

            with mark("qkv"):
                qkv_piece(span, 0, p)
        for p in range(PIECES):
            share(span, p).wait_send()

    def layer(span, slot):
        mean = jnp.sum(squares[...], axis=-1, keepdims=True) / width
        scale = lax.rsqrt(mean + tiny)
        queries = (acc[:, :hd] * scale).astype(bf16)
        kv[slot, 0] = (acc[:, hd : 2 * hd] * scale).astype(bf16)
        kv[slot, 1] = (acc[:, 2 * hd :] * scale).astype(bf16)

        @pl.when(span == 0)
        def _():
            load(1, slot).wait()
            with mark("round"):
                round_weights(slot)
            load(2, slot).wait()

        if slot == 1:

            @pl.when(span == 1)
            def _():
                with mark("finish1"):
                    finish_weights(1, 1)
                    finish_weights(1, 2)

            @pl.when((span == 1) & early)
            def _():
                for m in range(3):
                    rs1_open(0, m)

        with mark("qmap"):
            gate = dot(queries, wb[slot, 0]) * head_scale
            lift = dot(queries, wb[slot, 1]) * head_scale
            hidden = (gate * jax.nn.sigmoid(gate) * lift).astype(bf16)
            answer = dot(hidden, wb[slot, 2], ((1,), (1,))) * head_scale
            answer_mean = jnp.mean(answer * answer, axis=-1, keepdims=True)
            normed_out = (answer * lax.rsqrt(answer_mean + tiny)).astype(bf16)

        with mark("outp"):
            for p in range(PIECES):
                for side in range(2):
                    psend[slot, p, side] = dot(normed_out, wout[slot, :, cols(p, side)])
                if p % 2 == 1:
                    mix(slot, p - 1).start()
                    mix(slot, p).start()

        with mark("kvpath"):
            keys = kv[slot, 0]
            values = kv[slot, 1]
            gate = dot(keys, wb[slot, 0]) * head_scale
            lift = dot(keys, wb[slot, 1]) * head_scale
            up = dot(values, wb[slot, 2]) * (-head_scale)
            logistic = jax.nn.sigmoid(gate)
            act = gate * logistic
            grads[0] = (up * lift * (logistic * (1.0 + gate * (1.0 - logistic)))).astype(bf16)
            grads[1] = (up * act).astype(bf16)
            grads[2] = (act * lift).astype(bf16)

        with mark("gdots"):
            for m in range(3):
                terms = kv[slot, 0 if m < 2 else 1]
                sign = head_scale if m < 2 else -head_scale
                for e in range(2):
                    part = dot(terms, grads[m, :, e * 256 : (e + 1) * 256], ((0,), (0,))) * sign
                    for f in range(2):
                        gq[slot, m, 2 * e + f] = part[:, f * 128 : (f + 1) * 128].reshape(
                            gq.shape[3:]
                        )
        if slot == 0:

            @pl.when((span == 0) | jnp.logical_not(early))
            def _():
                for m in range(3):
                    rs1_open(slot, m)

        if slot == 0:

            @pl.when(span == 0)
            def _():
                load(0, 1).wait()

        for p in range(PIECES):
            with mark("mixwait"):
                mix(slot, p).wait_recv()
            old = xin[span, p]
            new = old + (psend[slot, p] + precv[slot, p])
            xin[span, p] = jnp.where(kept(slot, new.shape), new, old)

            def leave():
                @pl.when(s < sections - 1)
                def _():
                    hand_up(span, p).start()

                result(span, p).start()

            def go_on():
                with mark("qkv"):
                    qkv_piece(span, 1, p)

            if slot == 0:
                on(two, go_on)
                on(one, leave)
            else:
                leave()
        for p in range(PIECES):
            mix(slot, p).wait_send()

    def run_plan(span, plan):
        def stage(name, unit):
            slot, m = unit // 3, unit % 3
            only_first = {"D": ag1_open, "E": ag2_open, "F": ag2_pass, "H": finish_weights}
            always = {"A": rs1_open, "B": rs1_pass, "C": rs1_close, "D": rs2_close}
            with mark(name + str(unit)):
                if name in always:
                    always[name](slot, m)
                if name in only_first:
                    on(span == 0, lambda: only_first[name](slot, m))

        for step in plan:
            stage(step[0], int(step[1]))

    def phase(k, carry):
        span = jnp.minimum(k, 1)

        now = (k == 0) | ((k == 1) & early) | ((k == 2) & jnp.logical_not(early))

        @pl.when(now)
        def _():
            arrive(span)

        @pl.when((k == 1) & two)
        def _():
            run_plan(0, PLAN_MIDDLE)

        @pl.when(now)
        def _():
            layer(span, 0)

        @pl.when((k != 1) & two)
        def _():
            layer(span, 1)
            run_plan(span, PLAN_TWO)

        @pl.when((k == 1) & two)
        def _():
            run_plan(0, PLAN_TAIL)

        if two is not True:

            @pl.when((k != 1) & one)
            def _():
                run_plan(span, PLAN_ONE)

        return carry

    lax.fori_loop(0, 3, phase, 0)
    for m in range(3):
        rs_sent(0, m)

    def second_sent():
        for m in range(3):
            rs_sent(1, m)

    on(two, second_sent)

    if two is not True:

        @pl.when(one)
        def _():
            load(1, 1).wait()
            load(2, 1).wait()

    def stats(dy, dx):
        k = dy * SIDE + dx
        to = {"tok": turn(iy, dy) * SIDE + turn(ix, dx)}
        return remote(st, st_recv.at[k], st_sem.at[0], st_sem.at[1], to)

    others = [(dy, dx) for dy in range(SIDE) for dx in range(SIDE) if dy or dx]
    st[...] = jnp.zeros(st.shape, f32)

    def own_squares(slot):
        for m in range(3):
            total = jnp.zeros((8, 128), f32)
            for q in range(QUARTERS):
                values = gt[slot, m, q, iy, ix]
                total = total + jnp.sum((values * values).reshape(-1, 8, 128), axis=0)
            u = slot * 3 + m
            st[u : u + 1, :] = jnp.sum(total, axis=0, keepdims=True)

    own_squares(0)
    on(two, lambda: own_squares(1))
    for dy, dx in others:
        stats(dy, dx).start()
    with mark("stats"):
        taken(st_recv.at[1:], st_sem.at[1])
    everyone = st[...]
    for dy, dx in others:
        everyone = everyone + st_recv[dy * SIDE + dx]
    mean = jnp.sum(everyone, axis=-1, keepdims=True) / (hd * hd)
    factors = step_rate * lax.rsqrt(mean + tiny)

    def final(slot, m):
        return pltpu.make_async_copy(wfast.at[slot, m, t], fin.at[slot, m], fin_sem.at[slot, m])

    def last_update(slot):
        for m in range(3):
            factor = factors[slot * 3 + m : slot * 3 + m + 1]
            for q in range(QUARTERS):
                old = wfast[slot, m, t, :, q * 128 : (q + 1) * 128]
                new = old - factor * gt[slot, m, q, iy, ix]
                wfast[slot, m, t, :, q * 128 : (q + 1) * 128] = jnp.where(
                    kept(slot, new.shape), new, old
                )

    last_update(0)
    on(two, lambda: last_update(1))
    for slot in range(2):
        for m in range(3):
            final(slot, m).start()
    for slot in range(2):
        for m in range(3):
            final(slot, m).wait()
    taken(st_recv.at[1:], st_sem.at[0])
    for span in range(2):
        for p in range(PIECES):
            result(span, p).wait()

            @pl.when(s < sections - 1)
            def _():
                hand_up(span, p).wait_send()


def body(stream, counts, norm_gain, w_qkv, w_out, fast_init):
    spans, rows, half = stream.shape
    slots, width, columns = w_qkv.shape[1:]
    hd = fast_init.shape[-1]
    toks = lax.axis_size("tok")
    share = hd // toks
    fast = fast_init.reshape(slots, 3, toks, share, hd)
    piece = half // PIECES
    dma = pltpu.SemaphoreType.DMA
    quarter = hd // QUARTERS
    anywhere = pl.BlockSpec(memory_space=pl.ANY)
    sections = lax.axis_size("segment")

    def specialised(pattern, *arrays):
        deep = tuple(
            i < sections - FREE or pattern >> (i - sections + FREE) & 1 == 1
            for i in range(sections)
        )
        return pl.pallas_call(
            functools.partial(kernel, deep),
            out_shape=(
                jax.ShapeDtypeStruct((spans, rows, half), f32),
                jax.ShapeDtypeStruct((slots, 3, share, hd), f32),
            ),
            in_specs=[
                anywhere,
                pl.BlockSpec(memory_space=pltpu.SMEM),
                pl.BlockSpec(memory_space=pltpu.VMEM),
                anywhere,
                anywhere,
                anywhere,
            ],
            out_specs=(anywhere, anywhere),
            scratch_shapes=[
                pltpu.VMEM((slots, width, columns), bf16),
                pltpu.VMEM((slots, hd, width), bf16),
                pltpu.VMEM((slots, 3, toks, share, hd), f32),
                pltpu.VMEM((slots, 3, hd, hd), bf16),
                pltpu.VMEM((spans, PIECES, 2, rows, piece), f32),
                pltpu.VMEM((rows, columns), f32),
                pltpu.VMEM((rows, piece), f32),
                pltpu.VMEM((slots, PIECES, 2, rows, piece), f32),
                pltpu.VMEM((slots, PIECES, 2, rows, piece), f32),
                pltpu.VMEM((slots, 2, rows, hd), bf16),
                pltpu.VMEM((3, rows, hd), bf16),
                pltpu.VMEM((slots, 3, QUARTERS, SIDE, SIDE, share, quarter), f32),
                pltpu.VMEM((slots, 3, QUARTERS, SIDE, SIDE, share, quarter), f32),
                pltpu.VMEM((slots, 3, QUARTERS, 3, SIDE, share, quarter), f32),
                pltpu.VMEM((slots, 3, QUARTERS, SIDE, share, quarter), f32),
                pltpu.VMEM((slots, 3, QUARTERS, 3, share, quarter), f32),
                pltpu.VMEM((8, 128), f32),
                pltpu.VMEM((SIDE * SIDE, 8, 128), f32),
                dma((3, slots)),
                dma((spans, PIECES)),
            ]
            + [dma((spans, PIECES)) for _ in range(4)]
            + [dma((slots, PIECES)) for _ in range(2)]
            + [dma((slots, 3, n)) for n in (2, 3, 2, 3)]
            + [dma((2,)), dma((spans, PIECES)), dma((slots, 3))],
            compiler_params=pltpu.CompilerParams(
                collective_id=pattern, has_side_effects=True, vmem_limit_bytes=67043328
            ),
        )(*arrays)

    powers = 2 ** jnp.arange(FREE, dtype=jnp.int32)
    pattern = jnp.clip(jnp.sum((counts[sections - FREE :] - 1) * powers), 0, 2**FREE - 1)
    branches = [functools.partial(specialised, p) for p in range(2**FREE)]
    res, fin = lax.switch(
        pattern, branches, stream, counts, norm_gain[0], w_qkv[0], w_out[0], fast
    )
    return (res[None], fin.reshape(1, slots, 1, 3, share, hd))


def solution(mesh):
    in_specs = (
        P(None, "tok", "head"),
        P(),
        P("segment", None, None),
        P("segment", None, None, "head"),
        P("segment", None, "head", None),
        P("segment", None, "head", None, None, None),
    )
    out_specs = (P("segment", None, "tok", "head"), P("segment", None, "head", None, "tok", None))
    return jax.shard_map(body, mesh=mesh, in_specs=in_specs, out_specs=out_specs, check_vma=False)
```

```python
import contextlib
import functools

import jax
import jax.numpy as jnp
from jax import lax
from jax.experimental import pallas as pl
from jax.experimental.pallas import tpu as pltpu
from jax.sharding import PartitionSpec as P

MESH = pl.DeviceIdType.MESH
step_rate = 0.5
tiny = 1e-06
SIDE = 4
QUARTERS = 4
FREE = 2
PIECES = 4
PLAN_TWO = (
    "B0", "A3", "B1", "A4", "B2", "A5", "C0", "B3", "C1", "B4", "K0", "C2", "B5", "K1", "D0",
    "C3", "K2", "C4", "D1", "L0", "C5", "K3", "D2", "K4", "L1", "E0", "K5", "D3", "L2", "D4",
    "E1", "D5", "L3", "F0", "E2", "L4", "L5", "E3", "F1", "E4", "F2", "E5", "H0", "F3", "H1",
)
PLAN_MIDDLE = (
    "F4", "H2", "F5",
)
PLAN_TAIL = (
    "H3",
)
PLAN_ONE = (
    "B0", "B1", "B2", "C0", "C1", "C2", "K0", "K1", "K2", "D0", "D1", "D2", "L0", "L1", "L2",
    "E0", "E1", "E2", "F0", "F1", "F2", "H0", "H1", "H2",
)


def mark(name):
    return contextlib.nullcontext()


f32 = jnp.float32
bf16 = jnp.bfloat16


def on(condition, run):
    if condition is True:
        run()
    elif condition is not False:
        pl.when(condition)(run)


def kernel(
    deep,
    stream, counts, gain, wqkv_hbm, wout_hbm, fast_hbm,
    res, fin,
    wqkv, wout, wfast, wb, xin, acc, squares, psend, precv, kv, grads,
    gq, gt, r1, s1, r2, st, st_recv,
    load_sem, x_load, x_send, x_recv, z_send, z_recv, p_send, p_recv,
    rs_send, rs_recv, ag_send, ag_recv,
    st_sem, res_sem, fin_sem,
):
    sections = lax.axis_size("segment")
    s = lax.axis_index("segment")
    t = lax.axis_index("tok")
    h = lax.axis_index("head")
    iy = t // SIDE
    ix = t % SIDE
    piece = xin.shape[4]
    half = piece * PIECES
    width = 2 * half
    hd = wout.shape[1]
    head_scale = hd ** (-0.5)

    def turn(i, d):
        return (i + d + SIDE) % SIDE

    def on_x(d):
        return {"tok": iy * SIDE + turn(ix, d)}

    def on_y(d):
        return {"tok": turn(iy, d) * SIDE + ix}

    partner = {"head": 1 - h}
    above = {"segment": (s + 1) % sections}
    below = {"segment": (s + sections - 1) % sections}

    def load(kind, slot):
        src, dst = ((wqkv_hbm, wqkv), (fast_hbm, wfast), (wout_hbm, wout))[kind]
        return pltpu.make_async_copy(src.at[slot], dst.at[slot], load_sem.at[kind, slot])

    def cols(p, side=0):
        return pl.ds(side * half + p * piece, piece)

    def load_x(span, p):
        return pltpu.make_async_copy(
            stream.at[span, :, cols(p)], xin.at[span, p, h], x_load.at[span, p]
        )

    @pl.when(s == 0)
    def _():
        for span in range(2):
            for p in range(PIECES):
                load_x(span, p).start()

    for slot in range(2):
        for kind in range(3):
            load(kind, slot).start()

    barrier = pltpu.get_barrier_semaphore()
    peers = [partner, above, below]
    for d in (1, 3):
        peers += [on_x(d), on_y(d)]
    for peer in peers:
        pl.semaphore_signal(barrier, inc=1, device_id=peer, device_id_type=MESH)
    pl.semaphore_wait(barrier, len(peers))

    def remote(src, dst, send, recv, device):
        return pltpu.make_async_remote_copy(
            src_ref=src, dst_ref=dst, send_sem=send, recv_sem=recv,
            device_id=device, device_id_type=MESH,
        )

    def hand_up(span, p):
        part = xin.at[span, p, h]
        return remote(part, part, z_send.at[span, p], z_recv.at[span, p], above)

    def share(span, p):
        part = xin.at[span, p, h]
        return remote(part, part, x_send.at[span, p], x_recv.at[span, p], partner)

    def share_in(span, p):
        part = xin.at[span, p, 1 - h]
        return remote(part, part, x_send.at[span, p], x_recv.at[span, p], partner)

    def mix(slot, p):
        return remote(
            psend.at[slot, p], precv.at[slot, p], p_send.at[slot, p], p_recv.at[slot, p], partner
        )

    def result(span, p):
        return pltpu.make_async_copy(
            xin.at[span, p, h], res.at[span, :, cols(p)], res_sem.at[span, p]
        )

    def order(q):
        forward = 1 if q % 2 == 0 else -1
        if q < 2:
            return forward, iy, on_y, ix, on_x
        return forward, ix, on_x, iy, on_y

    def line(buf, slot, m, q, j):
        return buf.at[slot, m, q, j] if q < 2 else buf.at[slot, m, q, :, j]

    def cell(buf, slot, m, q, j):
        if q < 2:
            return buf.at[slot, m, q, iy, j]
        return buf.at[slot, m, q, j, ix]

    def rs1(slot, m, q, k):
        d, i, to, _, _ = order(q)
        j = (turn(i, 2), turn(i, d), turn(i, -d))[k]
        return remote(
            line(gq, slot, m, q, j), r1.at[slot, m, q, k],
            rs_send.at[slot, m, 0], rs_recv.at[slot, m, min(k, 1)], to(d if k < 2 else -d),
        )

    def rs2(slot, m, q, k):
        d, _, _, i, to = order(q)
        j = (turn(i, 2), turn(i, d), turn(i, -d))[k]
        return remote(
            s1.at[slot, m, q, j], r2.at[slot, m, q, k],
            rs_send.at[slot, m, 1], rs_recv.at[slot, m, 2 + min(k, 1)], to(d if k < 2 else -d),
        )

    def ag1(slot, m, q, k):
        d, _, _, i, to = order(q)
        part = cell(gt, slot, m, q, (i, i, turn(i, -d))[k])
        return remote(
            part, part, ag_send.at[slot, m, 0], ag_recv.at[slot, m, min(k, 1)], to((d, -d, d)[k])
        )

    def ag2(slot, m, q, k):
        d, i, to, _, _ = order(q)
        part = line(gt, slot, m, q, (i, i, turn(i, -d))[k])
        return remote(
            part, part, ag_send.at[slot, m, 1], ag_recv.at[slot, m, 2 + min(k, 1)], to((d, -d, d)[k])
        )

    def taken(part, sem):
        pltpu.make_async_copy(part, part, sem).wait()

    def rs1_open(slot, m):
        for k in (0, 2):
            for q in range(QUARTERS):
                rs1(slot, m, q, k).start()

    def rs1_pass(slot, m):
        taken(r1.at[slot, m, :, 0], rs_recv.at[slot, m, 0])
        for q in range(QUARTERS):
            d, i, _, _, _ = order(q)
            block = line(gq, slot, m, q, turn(i, d))
            block[...] = block[...] + r1[slot, m, q, 0]
            rs1(slot, m, q, 1).start()

    def rs1_close(slot, m):
        taken(r1.at[slot, m, :, 1:], rs_recv.at[slot, m, 1])
        for q in range(QUARTERS):
            _, i, _, _, _ = order(q)
            s1[slot, m, q] = line(gq, slot, m, q, i)[...] + r1[slot, m, q, 1] + r1[slot, m, q, 2]
            rs2(slot, m, q, 0).start()
            rs2(slot, m, q, 2).start()

    def rs2_pass(slot, m):
        taken(r2.at[slot, m, :, 0], rs_recv.at[slot, m, 2])
        for q in range(QUARTERS):
            d, _, _, i, _ = order(q)
            block = s1.at[slot, m, q, turn(i, d)]
            block[...] = block[...] + r2[slot, m, q, 0]
            rs2(slot, m, q, 1).start()

    def rs2_close(slot, m):
        taken(r2.at[slot, m, :, 1:], rs_recv.at[slot, m, 3])
        for q in range(QUARTERS):
            _, _, _, i, _ = order(q)
            cell(gt, slot, m, q, i)[...] = (
                s1[slot, m, q, i] + r2[slot, m, q, 1] + r2[slot, m, q, 2]
            )

    def ag1_open(slot, m):
        for q in range(QUARTERS):
            ag1(slot, m, q, 0).start()
            ag1(slot, m, q, 1).start()

    def ag1_pass(slot, m):
        taken(r2.at[slot, m, :, 0], ag_recv.at[slot, m, 0])
        for q in range(QUARTERS):
            ag1(slot, m, q, 2).start()

    def ag2_open(slot, m):
        taken(r2.at[slot, m, :, 1:], ag_recv.at[slot, m, 1])
        for q in range(QUARTERS):
            ag2(slot, m, q, 0).start()
            ag2(slot, m, q, 1).start()

    def ag2_pass(slot, m):
        taken(r1.at[slot, m, :, 0], ag_recv.at[slot, m, 2])
        for q in range(QUARTERS):
            ag2(slot, m, q, 2).start()

    def ag2_close(slot, m):
        taken(r1.at[slot, m, :, 1:], ag_recv.at[slot, m, 3])

    def rs_sent(slot, m):
        taken(r1.at[slot, m], rs_send.at[slot, m, 0])
        taken(r2.at[slot, m], rs_send.at[slot, m, 1])

    def ag_sent(slot, m):
        taken(r2.at[slot, m], ag_send.at[slot, m, 0])
        taken(r1.at[slot, m], ag_send.at[slot, m, 1])

    def kept(slot, shape):
        return jnp.broadcast_to(counts[s], shape) > slot

    def update_weights(slot, m):
        def add_squares(b, total):
            part = total
            for q in range(QUARTERS):
                values = gt[slot, m, q, b]
                part = part + jnp.sum(values * values, axis=0)
            return part

        total = lax.fori_loop(0, SIDE, add_squares, jnp.zeros(gt.shape[-2:], f32))
        mean = jnp.sum(total, keepdims=True) / (hd * hd)
        factor = step_rate * lax.rsqrt(mean + tiny)

        def change(b, carry):
            for q in range(QUARTERS):
                lanes = pl.ds(q * 128, 128)
                old = wfast[slot, m, pl.ds(b * SIDE, SIDE), :, lanes]
                new = old - factor * gt[slot, m, q, b]
                new = jnp.where(kept(slot, new.shape), new, old)
                wfast[slot, m, pl.ds(b * SIDE, SIDE), :, lanes] = new
                height = SIDE * new.shape[1]
                wb[slot, m, pl.ds(b * height, height), lanes] = new.reshape(height, -1).astype(bf16)
            return carry

        lax.fori_loop(0, SIDE, change, 0)

    def round_weights(slot):
        for m in range(3):

            def one(b, carry):
                block = wfast[slot, m, pl.ds(b * SIDE, SIDE)]
                height = SIDE * block.shape[1]
                wb[slot, m, pl.ds(b * height, height)] = block.reshape(height, hd).astype(bf16)
                return carry

            lax.fori_loop(0, SIDE, one, 0)

    def finish_weights(slot, m):
        ag2_close(slot, m)
        update_weights(slot, m)
        ag_sent(slot, m)
        rs_sent(slot, m)

    def dot(a, b, dims=((1,), (0,))):
        return lax.dot_general(a, b, (dims, ((), ())), preferred_element_type=f32)

    two = True if all(deep) else sum((s == i).astype(jnp.int32) for i, d in enumerate(deep) if d) > 0
    one = False if two is True else jnp.logical_not(two)
    early = (s == 0) & two

    def qkv_piece(span, slot, p):
        low = xin[span, p, 0]
        high = xin[span, p, 1]
        both = low * low + high * high
        low = (low * gain[slot : slot + 1, cols(p)]).astype(bf16)
        high = (high * gain[slot : slot + 1, cols(p, 1)]).astype(bf16)
        terms = dot(low, wqkv[slot, cols(p)]) + dot(high, wqkv[slot, cols(p, 1)])
        squares[...] = both if p == 0 else squares[...] + both
        acc[...] = terms if p == 0 else acc[...] + terms

    def arrive(span):
        @pl.when(s == 0)
        def _():
            for p in range(PIECES):
                load_x(span, p).wait()
                share(span, p).start()

        for p in range(PIECES):

            @pl.when(s > 0)
            def _():
                with mark("hand"):
                    hand_up(span, p).wait_recv()
                share(span, p).start()

            with mark("share"):
                share_in(span, p).wait_recv()
            if p == 0:

                @pl.when(span == 0)
                def _():
                    load(0, 0).wait()

            with mark("qkv"):
                qkv_piece(span, 0, p)
        for p in range(PIECES):
            share(span, p).wait_send()

    def layer(span, slot):
        mean = jnp.sum(squares[...], axis=-1, keepdims=True) / width
        scale = lax.rsqrt(mean + tiny)
        queries = (acc[:, :hd] * scale).astype(bf16)
        kv[slot, 0] = (acc[:, hd : 2 * hd] * scale).astype(bf16)
        kv[slot, 1] = (acc[:, 2 * hd :] * scale).astype(bf16)

        @pl.when(span == 0)
        def _():
            load(1, slot).wait()
            with mark("round"):
                round_weights(slot)
            load(2, slot).wait()

        if slot == 1:

            @pl.when(span == 1)
            def _():
                with mark("finish1"):
                    finish_weights(1, 1)
                    finish_weights(1, 2)

            @pl.when((span == 1) & early)
            def _():
                for m in range(3):
                    rs1_open(0, m)

        with mark("qmap"):
            gate = dot(queries, wb[slot, 0]) * head_scale
            lift = dot(queries, wb[slot, 1]) * head_scale
            hidden = (gate * jax.nn.sigmoid(gate) * lift).astype(bf16)
            answer = dot(hidden, wb[slot, 2], ((1,), (1,))) * head_scale
            answer_mean = jnp.mean(answer * answer, axis=-1, keepdims=True)
            normed_out = (answer * lax.rsqrt(answer_mean + tiny)).astype(bf16)

        with mark("outp"):
            for p in range(PIECES):
                for side in range(2):
                    psend[slot, p, side] = dot(normed_out, wout[slot, :, cols(p, side)])
                if p % 2 == 1:
                    mix(slot, p - 1).start()
                    mix(slot, p).start()

        with mark("kvpath"):
            keys = kv[slot, 0]
            values = kv[slot, 1]
            gate = dot(keys, wb[slot, 0]) * head_scale
            lift = dot(keys, wb[slot, 1]) * head_scale
            up = dot(values, wb[slot, 2]) * (-head_scale)
            logistic = jax.nn.sigmoid(gate)
            act = gate * logistic
            grads[0] = (up * lift * (logistic * (1.0 + gate * (1.0 - logistic)))).astype(bf16)
            grads[1] = (up * act).astype(bf16)
            grads[2] = (act * lift).astype(bf16)

        with mark("gdots"):
            for m in range(3):
                terms = kv[slot, 0 if m < 2 else 1]
                sign = head_scale if m < 2 else -head_scale
                for e in range(2):
                    part = dot(terms, grads[m, :, e * 256 : (e + 1) * 256], ((0,), (0,))) * sign
                    for f in range(2):
                        gq[slot, m, 2 * e + f] = part[:, f * 128 : (f + 1) * 128].reshape(
                            gq.shape[3:]
                        )
        if slot == 0:

            @pl.when((span == 0) | jnp.logical_not(early))
            def _():
                for m in range(3):
                    rs1_open(slot, m)

        if slot == 0:

            @pl.when(span == 0)
            def _():
                load(0, 1).wait()

        for p in range(PIECES):
            with mark("mixwait"):
                mix(slot, p).wait_recv()
            old = xin[span, p]
            new = old + (psend[slot, p] + precv[slot, p])
            xin[span, p] = jnp.where(kept(slot, new.shape), new, old)

            def leave():
                @pl.when(s < sections - 1)
                def _():
                    hand_up(span, p).start()

                result(span, p).start()

            def go_on():
                with mark("qkv"):
                    qkv_piece(span, 1, p)

            if slot == 0:
                on(two, go_on)
                on(one, leave)
            else:
                leave()
        for p in range(PIECES):
            mix(slot, p).wait_send()

    def run_plan(span, plan):
        def stage(name, unit):
            slot, m = unit // 3, unit % 3
            only_first = {
                "D": ag1_open, "L": ag1_pass, "E": ag2_open, "F": ag2_pass, "H": finish_weights,
            }
            always = {
                "A": rs1_open, "B": rs1_pass, "C": rs1_close, "K": rs2_pass, "D": rs2_close,
            }
            with mark(name + str(unit)):
                if name in always:
                    always[name](slot, m)
                if name in only_first:
                    on(span == 0, lambda: only_first[name](slot, m))

        for step in plan:
            stage(step[0], int(step[1]))

    def phase(k, carry):
        span = jnp.minimum(k, 1)

        now = (k == 0) | ((k == 1) & early) | ((k == 2) & jnp.logical_not(early))

        @pl.when(now)
        def _():
            arrive(span)

        @pl.when((k == 1) & two)
        def _():
            run_plan(0, PLAN_MIDDLE)

        @pl.when(now)
        def _():
            layer(span, 0)

        @pl.when((k != 1) & two)
        def _():
            layer(span, 1)
            run_plan(span, PLAN_TWO)

        @pl.when((k == 1) & two)
        def _():
            run_plan(0, PLAN_TAIL)

        if two is not True:

            @pl.when((k != 1) & one)
            def _():
                run_plan(span, PLAN_ONE)

        return carry

    lax.fori_loop(0, 3, phase, 0)
    for m in range(3):
        rs_sent(0, m)

    def second_sent():
        for m in range(3):
            rs_sent(1, m)

    on(two, second_sent)

    if two is not True:

        @pl.when(one)
        def _():
            load(1, 1).wait()
            load(2, 1).wait()

    def stats(dy, dx):
        k = dy * SIDE + dx
        to = {"tok": turn(iy, dy) * SIDE + turn(ix, dx)}
        return remote(st, st_recv.at[k], st_sem.at[0], st_sem.at[1], to)

    others = [(dy, dx) for dy in range(SIDE) for dx in range(SIDE) if dy or dx]
    st[...] = jnp.zeros(st.shape, f32)

    def own_squares(slot):
        for m in range(3):
            total = jnp.zeros((8, 128), f32)
            for q in range(QUARTERS):
                values = gt[slot, m, q, iy, ix]
                total = total + jnp.sum((values * values).reshape(-1, 8, 128), axis=0)
            u = slot * 3 + m
            st[u : u + 1, :] = jnp.sum(total, axis=0, keepdims=True)

    own_squares(0)
    on(two, lambda: own_squares(1))
    for dy, dx in others:
        stats(dy, dx).start()
    with mark("stats"):
        taken(st_recv.at[1:], st_sem.at[1])
    everyone = st[...]
    for dy, dx in others:
        everyone = everyone + st_recv[dy * SIDE + dx]
    mean = jnp.sum(everyone, axis=-1, keepdims=True) / (hd * hd)
    factors = step_rate * lax.rsqrt(mean + tiny)

    def final(slot, m):
        return pltpu.make_async_copy(wfast.at[slot, m, t], fin.at[slot, m], fin_sem.at[slot, m])

    def last_update(slot):
        for m in range(3):
            factor = factors[slot * 3 + m : slot * 3 + m + 1]
            for q in range(QUARTERS):
                old = wfast[slot, m, t, :, q * 128 : (q + 1) * 128]
                new = old - factor * gt[slot, m, q, iy, ix]
                wfast[slot, m, t, :, q * 128 : (q + 1) * 128] = jnp.where(
                    kept(slot, new.shape), new, old
                )

    last_update(0)
    on(two, lambda: last_update(1))
    for slot in range(2):
        for m in range(3):
            final(slot, m).start()
    for slot in range(2):
        for m in range(3):
            final(slot, m).wait()
    taken(st_recv.at[1:], st_sem.at[0])
    for span in range(2):
        for p in range(PIECES):
            result(span, p).wait()

            @pl.when(s < sections - 1)
            def _():
                hand_up(span, p).wait_send()


def body(stream, counts, norm_gain, w_qkv, w_out, fast_init):
    spans, rows, half = stream.shape
    slots, width, columns = w_qkv.shape[1:]
    hd = fast_init.shape[-1]
    toks = lax.axis_size("tok")
    share = hd // toks
    fast = fast_init.reshape(slots, 3, toks, share, hd)
    piece = half // PIECES
    dma = pltpu.SemaphoreType.DMA
    quarter = hd // QUARTERS
    anywhere = pl.BlockSpec(memory_space=pl.ANY)
    sections = lax.axis_size("segment")

    def specialised(pattern, *arrays):
        deep = tuple(
            i < sections - FREE or pattern >> (i - sections + FREE) & 1 == 1
            for i in range(sections)
        )
        return pl.pallas_call(
            functools.partial(kernel, deep),
            out_shape=(
                jax.ShapeDtypeStruct((spans, rows, half), f32),
                jax.ShapeDtypeStruct((slots, 3, share, hd), f32),
            ),
            in_specs=[
                anywhere,
                pl.BlockSpec(memory_space=pltpu.SMEM),
                pl.BlockSpec(memory_space=pltpu.VMEM),
                anywhere,
                anywhere,
                anywhere,
            ],
            out_specs=(anywhere, anywhere),
            scratch_shapes=[
                pltpu.VMEM((slots, width, columns), bf16),
                pltpu.VMEM((slots, hd, width), bf16),
                pltpu.VMEM((slots, 3, toks, share, hd), f32),
                pltpu.VMEM((slots, 3, hd, hd), bf16),
                pltpu.VMEM((spans, PIECES, 2, rows, piece), f32),
                pltpu.VMEM((rows, columns), f32),
                pltpu.VMEM((rows, piece), f32),
                pltpu.VMEM((slots, PIECES, 2, rows, piece), f32),
                pltpu.VMEM((slots, PIECES, 2, rows, piece), f32),
                pltpu.VMEM((slots, 2, rows, hd), bf16),
                pltpu.VMEM((3, rows, hd), bf16),
                pltpu.VMEM((slots, 3, QUARTERS, SIDE, SIDE, share, quarter), f32),
                pltpu.VMEM((slots, 3, QUARTERS, SIDE, SIDE, share, quarter), f32),
                pltpu.VMEM((slots, 3, QUARTERS, 3, SIDE, share, quarter), f32),
                pltpu.VMEM((slots, 3, QUARTERS, SIDE, share, quarter), f32),
                pltpu.VMEM((slots, 3, QUARTERS, 3, share, quarter), f32),
                pltpu.VMEM((8, 128), f32),
                pltpu.VMEM((SIDE * SIDE, 8, 128), f32),
                dma((3, slots)),
                dma((spans, PIECES)),
            ]
            + [dma((spans, PIECES)) for _ in range(4)]
            + [dma((slots, PIECES)) for _ in range(2)]
            + [dma((slots, 3, n)) for n in (2, 4, 2, 4)]
            + [dma((2,)), dma((spans, PIECES)), dma((slots, 3))],
            compiler_params=pltpu.CompilerParams(
                collective_id=pattern, has_side_effects=True, vmem_limit_bytes=67043328
            ),
        )(*arrays)

    powers = 2 ** jnp.arange(FREE, dtype=jnp.int32)
    pattern = jnp.clip(jnp.sum((counts[sections - FREE :] - 1) * powers), 0, 2**FREE - 1)
    branches = [functools.partial(specialised, p) for p in range(2**FREE)]
    res, fin = lax.switch(
        pattern, branches, stream, counts, norm_gain[0], w_qkv[0], w_out[0], fast
    )
    return (res[None], fin.reshape(1, slots, 1, 3, share, hd))


def solution(mesh):
    in_specs = (
        P(None, "tok", "head"),
        P(),
        P("segment", None, None),
        P("segment", None, None, "head"),
        P("segment", None, "head", None),
        P("segment", None, "head", None, None, None),
    )
    out_specs = (P("segment", None, "tok", "head"), P("segment", None, "head", None, "tok", None))
    return jax.shard_map(body, mesh=mesh, in_specs=in_specs, out_specs=out_specs, check_vma=False)
```
